32 devices in a mesh: groups: 2 (over y), tok: 4 (over z), cache: 2 (over x), rep: 2 (over core).
Axes of the slice: x: 2, y: 2, z: 4, core: 2. Of those that a mesh axis runs over, the one named last changes fastest.
Arguments:
- x_in: bfloat16 [16, 512, 8192], P(('groups', 'rep'), 'tok', 'cache'), parts along dimension 0, may hold values from -6 to 6
- z_in: bfloat16 [16, 512, 8192], P(('groups', 'rep'), 'tok', 'cache'), parts along dimension 0, may hold values from -6 to 6
- b_in: bfloat16 [16, 512, 8, 128], P(('groups', 'rep'), 'tok', 'cache'), parts along dimension 0, may hold values from -6 to 6
- c_in: bfloat16 [16, 512, 8, 128], P(('groups', 'rep'), 'tok', 'cache'), parts along dimension 0, may hold values from -6 to 6
- dt_in: bfloat16 [16, 512, 128], P(('groups', 'rep'), 'tok', 'cache'), parts along dimension 0, may hold values from -2 to 10
- dt_bias: float32 [128], P('cache'), may hold values from -14 to -2
- a_log: float32 [128], P('cache'), may hold values from 0 to 3
- skip_gain: float32 [128], P('cache'), may hold values from 0.5 to 1.5
- norm_w: float32 [8192], P('cache'), may hold values from 0.5 to 1.5
- cache_states: float32 [8, 2, 64, 64, 128], P(('groups', 'cache'), None, 'tok'), parts along dimension 0, may hold values from -0.3 to 0.3
- parent: int32 [16], P('groups'), parts along dimension 0, may hold values from 0 to 3
- state_dev: int32 [8], P('groups'), parts along dimension 0, may hold values from 0 to 1, as said below
- state_slot: int32 [8], P('groups'), parts along dimension 0, may hold values from 0 to 1
- spans: int32 [16], P('groups'), parts along dimension 0, may hold values from 1 to 4
Outputs:
- y_out: bfloat16 [16, 512, 8192], P(('groups', 'rep'), 'tok', 'cache'), parts along dimension 0
- final_states: float32 [16, 128, 64, 128], P(('groups', 'rep'), ('cache', 'tok')), parts along dimension 0
The draws below stay inside these ranges and needn't reach their ends.
There are 2 independent parts, one for each index of `groups`. The reference program is written for one: setup_inputs(seed, part) draws one part's arguments, and reference() takes and returns one part's arrays. A program takes and returns all parts, laid end to end along the dimension named above; an argument that names none is the same for every part. Nothing has to cross between parts.
Inputs may be any that keep to these rules, and one draw needn't show every extreme that they name: state_dev and state_slot together name every pair of a cache index and a slot exactly once.
All inputs are finite; a program needn't handle non-finite values.
Results may differ from the reference program's by a relative error of at most 0.0075.
Values may be sent and summed in bfloat16 or wider, within the bound.
No kernel may reach another device: no remote copies, remote signals or barrier semaphores. Data moves between devices by JAX's collectives and lax.ppermute only.
A program may use at most 128 MiB of HBM per device.

```python
import math
import jax
import jax.numpy as jnp
import numpy as np
from jax import lax

HEADS = 128
HEAD_DIM = 64
STATE = 128
GROUPS = 8
SPAN = 128
SLOTS_DEV = 2
HOLDERS = 2
BATCH_QUERIES = 8
QUERY_EXTENT = 512
NCHUNK = 4
KEPT = 4


def per_head_rates(key):
    time_scale = jnp.exp(jax.random.uniform(jax.random.fold_in(key, 31), (HEADS,), jnp.float32, 0.0, math.log(16.0)))
    slow_share = 0.55
    is_slow = jax.random.uniform(jax.random.fold_in(key, 32), (HEADS,), jnp.float32) < slow_share
    spread_draw = jax.random.uniform(jax.random.fold_in(key, 33), (HEADS,), jnp.float32)
    slow_rate = 0.3 * jnp.exp(spread_draw * math.log(1.0 / 0.3)) / QUERY_EXTENT
    fast_rate = jnp.exp(spread_draw * math.log(2.5)) / 50.0
    head_rate = jnp.where(is_slow, slow_rate, fast_rate)
    return (time_scale, head_rate)


def draw_a_log(key, part):
    time_scale, head_rate = per_head_rates(key)
    return jnp.log(time_scale).astype(jnp.float32)


def draw_dt_bias(key, part):
    time_scale, head_rate = per_head_rates(key)
    return jnp.log(jnp.expm1(head_rate / time_scale)).astype(jnp.float32)


def draw_dt_in(key, part):
    full_shape = (BATCH_QUERIES, QUERY_EXTENT, HEADS)
    jitter = jnp.clip(0.5 * jax.random.normal(jax.random.fold_in(key, 41), full_shape, jnp.float32), -2.0, 2.0)
    spurt_index = jax.random.randint(jax.random.fold_in(key, 42), (BATCH_QUERIES, 2), 0, QUERY_EXTENT)
    flagged_entries = jnp.any(jnp.arange(QUERY_EXTENT)[None, :, None] == spurt_index[:, None, :], axis=2)
    raw_value = jitter + math.log(QUERY_EXTENT / 2.0) * flagged_entries.astype(jnp.float32)[:, :, None]
    return raw_value.astype(jnp.bfloat16)


def kept_places(key):
    shuffled = jax.random.permutation(jax.random.fold_in(key, 51), KEPT)
    return (shuffled // SLOTS_DEV, shuffled % SLOTS_DEV)


def draw_state_dev(key, part):
    return kept_places(key)[0].astype(jnp.int32)


def draw_state_slot(key, part):
    return kept_places(key)[1].astype(jnp.int32)


def draw_spans(key, part):
    drawn_counts = jax.random.randint(jax.random.fold_in(key, 61), (BATCH_QUERIES,), 1, NCHUNK + 1)
    longest = jax.random.randint(jax.random.fold_in(key, 62), (), 0, BATCH_QUERIES)
    return jnp.where(jnp.arange(BATCH_QUERIES) == longest, NCHUNK, drawn_counts).astype(jnp.int32)


def place_ends(values, key, least, largest):
    longest = values.shape.index(max(values.shape))
    spots = []
    for shift in (0, 1):
        where = [jax.random.randint(jax.random.fold_in(key, axis), (), 0, length) for axis, length in enumerate(values.shape)]
        where[longest] = (where[longest] + shift) % values.shape[longest]
        spots.append(tuple(where))
    return values.at[spots[0]].set(least).at[spots[1]].set(largest)


def levels(stream_key, extent, cuts, least, largest):
    loudness = 1.0
    for dim, shards_of in cuts:
        heights = jax.random.uniform(jax.random.fold_in(jax.random.fold_in(stream_key, 6), dim), (shards_of,), jnp.float32, least / len(cuts), largest / len(cuts))
        loudness = loudness * jnp.repeat(jnp.exp(heights), extent[dim] // shards_of).reshape((-1,) + (1,) * (len(extent) - 1 - dim))
    return loudness


def rank_table(amount, skew):
    weights = [(1 << 20) // math.isqrt(standing ** skew) + 1 for standing in range(1, amount + 1)]
    width = 1 + sum(weights) // (1 << 30)
    return np.cumsum(np.array([max(1, weight // width) for weight in weights]))


def ranked(rng, dims, number_of, lean):
    grid = rank_table(number_of, lean)
    pick = jax.random.randint(jax.random.fold_in(rng, 1), dims, 0, int(grid[number_of - 1]))
    rank = jnp.searchsorted(jnp.asarray(grid, jnp.int32), pick, side="right")
    return jax.random.permutation(jax.random.fold_in(rng, 2), number_of)[rank].astype(jnp.int32)


def noise(stream_key, extent, width, most, split=(), held_as=jnp.bfloat16):
    drawn = width * jax.random.normal(stream_key, extent, jnp.float32)
    if split:
        drawn = drawn * levels(stream_key, extent, split, -0.22, 0.18)
    return jnp.clip(drawn, -most, most).astype(held_as)


def setup_inputs(seed: int = 0, part: int = 0) -> dict:
    arg_keys = jax.random.split(jax.random.key(seed), 15)
    part_keys = jax.random.split(jax.random.fold_in(arg_keys[14], part), 15)
    return {
        "x_in": noise(part_keys[0], (BATCH_QUERIES, QUERY_EXTENT, HEADS * HEAD_DIM), 1.0, 6.0, ((0, 2), (1, 4), (2, 2))),
        "z_in": noise(part_keys[1], (BATCH_QUERIES, QUERY_EXTENT, HEADS * HEAD_DIM), 1.0, 6.0, ((0, 2), (1, 4), (2, 2))),
        "b_in": noise(part_keys[2], (BATCH_QUERIES, QUERY_EXTENT, GROUPS, STATE), 1.0, 6.0, ((0, 2), (1, 4), (2, 2))),
        "c_in": noise(part_keys[3], (BATCH_QUERIES, QUERY_EXTENT, GROUPS, STATE), 1.0, 6.0, ((0, 2), (1, 4), (2, 2))),
        "dt_in": draw_dt_in(jax.random.fold_in(jax.random.fold_in(arg_keys[14], part), 71), part),
        "dt_bias": draw_dt_bias(jax.random.fold_in(arg_keys[14], 71), part),
        "a_log": draw_a_log(jax.random.fold_in(arg_keys[14], 71), part),
        "skip_gain": jnp.clip(0.5 + 1.0 * jax.random.uniform(arg_keys[7], (HEADS,), jnp.float32) ** levels(arg_keys[7], (HEADS,), ((0, 2),), -0.2, 0.2), 0.5, 1.5),
        "norm_w": jnp.clip(1.0 + 0.1 * jax.random.normal(arg_keys[8], (HEADS * HEAD_DIM,), jnp.float32), 0.5, 1.5),
        "cache_states": noise(part_keys[9], (KEPT, HOLDERS, HEADS // HOLDERS, HEAD_DIM, STATE), 0.05, 0.3, ((0, 2), (2, 4)), jnp.float32),
        "parent": place_ends(ranked(part_keys[10], (BATCH_QUERIES,), KEPT, 2), jax.random.fold_in(part_keys[10], 3), 0, KEPT - 1).astype(jnp.int32),
        "state_dev": draw_state_dev(jax.random.fold_in(jax.random.fold_in(arg_keys[14], part), 71), part),
        "state_slot": draw_state_slot(jax.random.fold_in(jax.random.fold_in(arg_keys[14], part), 71), part),
        "spans": draw_spans(jax.random.fold_in(jax.random.fold_in(arg_keys[14], part), 71), part),
    }


EPS = 1e-05

def one_request(inputs, dt_bias, a_log, skip_gain, norm_w):
    x_row, z_row, b_row, c_row, raw_row, interval_total, initial = inputs
    head_count = raw_row.shape[1]
    groups = b_row.shape[1]
    per_group = head_count // groups
    blocks = QUERY_EXTENT // SPAN
    valid_mask = (jnp.arange(QUERY_EXTENT) < interval_total * SPAN).astype(jnp.float32)
    step_size = jax.nn.softplus(raw_row.astype(jnp.float32) + dt_bias) * valid_mask[:, None]
    step_blocks = step_size.reshape(blocks, SPAN, head_count).transpose(0, 2, 1)
    cum_rate = jnp.cumsum(-jnp.exp(a_log)[:, None] * step_blocks, axis=2)
    b_blocks = b_row.reshape(blocks, SPAN, groups, STATE).astype(jnp.float32)
    c_blocks = c_row.reshape(blocks, SPAN, groups, STATE).astype(jnp.float32)
    x_blocks = x_row.reshape(blocks, SPAN, head_count, HEAD_DIM).astype(jnp.float32)
    scores = jnp.repeat(jnp.einsum('kign,kjgn->kgij', c_blocks, b_blocks), per_group, axis=1)
    causal = jnp.arange(SPAN)[:, None] >= jnp.arange(SPAN)[None, :]
    spread = cum_rate[:, :, :, None] - cum_rate[:, :, None, :]
    decay_mask = jnp.where(causal, jnp.exp(jnp.where(causal, spread, 0.0)), 0.0)
    blend_factors = (scores * decay_mask * step_blocks[:, :, None, :]).astype(jnp.bfloat16)
    diagonal = jnp.einsum('khij,kjhp->kihp', blend_factors.astype(jnp.float32), x_blocks)
    weight = jnp.exp(cum_rate[:, :, -1:] - cum_rate) * step_blocks
    b_heads = jnp.repeat(b_blocks, per_group, axis=2)
    scaled = (b_heads * weight.transpose(0, 2, 1)[..., None]).astype(jnp.bfloat16)
    block_states = jnp.einsum('kjhp,kjhn->khpn', x_blocks, scaled.astype(jnp.float32))
    running_totals = cum_rate[:, :, -1]

    def advance(carried, step_inputs):
        block_total, new_state = step_inputs
        return (jnp.exp(block_total)[:, None, None] * carried + new_state, carried)
    final_state, before = lax.scan(advance, initial, (running_totals, block_states))
    before_grouped = before.reshape(blocks, groups, per_group, HEAD_DIM, STATE)
    carried_in = jnp.einsum('kign,kgepn->kigep', c_blocks, before_grouped, precision=lax.Precision.HIGHEST)
    carried_in = carried_in.reshape(blocks, SPAN, head_count, HEAD_DIM)
    growth = jnp.exp(cum_rate).transpose(0, 2, 1)[..., None]
    ssd = (diagonal + carried_in * growth + skip_gain[:, None] * x_blocks).astype(jnp.bfloat16)
    gated = ssd.reshape(QUERY_EXTENT, head_count * HEAD_DIM).astype(jnp.float32) * jax.nn.silu(z_row.astype(jnp.float32))
    grouped = gated.reshape(QUERY_EXTENT, groups, -1)
    inverse_rms = lax.rsqrt(lax.optimization_barrier(jnp.mean(grouped * grouped, axis=-1, keepdims=True)) + EPS)
    result = (grouped * inverse_rms).reshape(QUERY_EXTENT, -1) * norm_w * valid_mask[:, None]
    return (result.astype(jnp.bfloat16), final_state)

def reference(x_in, z_in, b_in, c_in, dt_in, dt_bias, a_log, skip_gain, norm_w, cache_states, parent, state_dev, state_slot, spans):
    kept_rows = state_dev[parent] * SLOTS_DEV + state_slot[parent]
    initial = cache_states[kept_rows].reshape(BATCH_QUERIES, HEADS, HEAD_DIM, STATE)

    def handle(inputs):
        return one_request(inputs, dt_bias, a_log, skip_gain, norm_w)
    y_out, final_states = lax.map(handle, (x_in, z_in, b_in, c_in, dt_in, spans, initial))
    return (y_out, final_states)
```

```python
import functools

import jax
import jax.numpy as jnp
from jax import lax
from jax.experimental import pallas as pl
from jax.experimental.pallas import tpu as pltpu
from jax.sharding import PartitionSpec as P

HEADS = 128
HEAD_DIM = 64
GROUPS = 8
STATE = 128
SPAN = 128
EPS = 1e-05

PER_GROUP = HEADS // GROUPS
GROUP_LANES = PER_GROUP * HEAD_DIM
PAIR_LANES = 2 * HEAD_DIM
PAIRS = PER_GROUP // 2
REQ_CHUNK = 2
HOP = 2

F32 = jnp.float32
BF16 = jnp.bfloat16


def cost(flops, nbytes, trans=0):
    return pl.CostEstimate(flops=flops, bytes_accessed=nbytes, transcendentals=trans)


def low_half(rows):
    return lax.broadcasted_iota(jnp.int32, (rows, PAIR_LANES), 1) < HEAD_DIM


def spread_pair(values, q, low):
    return jnp.where(low, values[:, 2 * q : 2 * q + 1], values[:, 2 * q + 1 : 2 * q + 2])


def prep_body(valid_ref, dt_ref, bias_ref, alog_ref, cum_ref, cum_t_ref, step_t_ref, weight_ref, growth_ref, total_ref):
    requests, span, heads_here = dt_ref.shape
    rows = lax.broadcasted_iota(jnp.int32, (span, span), 0)
    cols = lax.broadcasted_iota(jnp.int32, (span, span), 1)
    lower = (rows >= cols).astype(F32)
    rate = -jnp.exp(alog_ref[...])
    for r in range(requests):
        raw = dt_ref[r].astype(F32) + bias_ref[...]
        positive = jnp.maximum(raw, 0.0) + jnp.log1p(jnp.exp(-jnp.abs(raw)))
        step = positive * valid_ref[r].astype(F32)
        cum = jnp.dot(lower, rate * step, precision=lax.Precision.HIGHEST, preferred_element_type=F32)
        total = cum[span - 1 : span, :]
        weight = jnp.exp(total - cum) * step
        growth = jnp.exp(cum)
        total_ref[r] = total
        cum_t = cum.T
        step_t = step.T
        for g in range(heads_here // PER_GROUP):
            here = slice(g * PER_GROUP, (g + 1) * PER_GROUP)
            cum_ref[r, g] = cum[:, here]
            weight_ref[r, g] = weight[:, here]
            growth_ref[r, g] = growth[:, here]
            cum_t_ref[r, g] = cum_t[here, :]
            step_t_ref[r, g] = step_t[here, :]


def prepare(valid, dt_in, bias, a_log):
    requests, span, heads_here = dt_in.shape
    groups = heads_here // PER_GROUP
    columns = jax.ShapeDtypeStruct((requests, groups, span, PER_GROUP), F32)
    as_rows = jax.ShapeDtypeStruct((requests, groups, PER_GROUP, span), F32)
    vmem = pl.BlockSpec(memory_space=pltpu.VMEM)
    return pl.pallas_call(
        prep_body,
        out_shape=(columns, as_rows, as_rows, columns, columns, jax.ShapeDtypeStruct((requests, 1, heads_here), F32)),
        in_specs=[pl.BlockSpec(memory_space=pltpu.SMEM), vmem, vmem, vmem],
        out_specs=(vmem,) * 6,
        cost_estimate=cost(20_000_000, 4_000_000),
        name="prep",
    )(valid, dt_in, bias, a_log)


def block_body(x_ref, b_ref, weight_ref, out_ref):
    weight = weight_ref[...].reshape(weight_ref.shape[-2:])
    low = low_half(weight.shape[0])
    scaled = []
    for q in range(PAIRS):
        lanes = slice(q * PAIR_LANES, (q + 1) * PAIR_LANES)
        scaled.append((x_ref[0, :, lanes].astype(F32) * spread_pair(weight, q, low)).astype(BF16))
    scaled = jnp.concatenate(scaled, axis=1)
    states = lax.dot_general(b_ref[0], scaled, (((0,), (0,)), ((), ())), preferred_element_type=F32)
    out_ref[...] = states.astype(BF16).reshape(out_ref.shape)


def block_states(x_in, b_flat, weight):
    requests, span, width = x_in.shape
    groups = width // GROUP_LANES
    parts = requests // REQ_CHUNK

    def at(i, j):
        return ((i % parts) * REQ_CHUNK + j, (i // parts + 1) % groups)

    return pl.pallas_call(
        block_body,
        grid=(groups * parts, REQ_CHUNK),
        out_shape=jax.ShapeDtypeStruct((groups * parts, REQ_CHUNK, STATE, GROUP_LANES), BF16),
        in_specs=[
            pl.BlockSpec((1, span, GROUP_LANES), lambda i, j: (at(i, j)[0], 0, at(i, j)[1])),
            pl.BlockSpec((1, span, STATE), lambda i, j: (at(i, j)[0], 0, at(i, j)[1])),
            pl.BlockSpec((1, 1, span, PER_GROUP), lambda i, j: (at(i, j)[0], at(i, j)[1], 0, 0)),
        ],
        out_specs=pl.BlockSpec((1, 1, STATE, GROUP_LANES), lambda i, j: (i, j, 0, 0)),
        cost_estimate=cost(600_000_000, 12_000_000),
        name="block_states",
    )(x_in, b_flat, weight)


def local_body(valid_ref, x_ref, b_ref, c_ref, cum_ref, cum_t_ref, step_t_ref, skip_ref, out_ref):
    span = x_ref.shape[1]

    @pl.when(valid_ref[pl.program_id(0)] > 0)
    def _():
        rows = lax.broadcasted_iota(jnp.int32, (span, span), 0)
        cols = lax.broadcasted_iota(jnp.int32, (span, span), 1)
        causal = rows >= cols
        low = low_half(span)
        scores = lax.dot_general(c_ref[0], b_ref[0], (((1,), (1,)), ((), ())), preferred_element_type=F32)
        cum = cum_ref[0, 0]
        cum_t = cum_t_ref[0, 0]
        step_t = step_t_ref[0, 0]

        def mix(h):
            spread = cum[:, h : h + 1] - cum_t[h : h + 1, :]
            decay = jnp.exp(jnp.where(causal, spread, -jnp.inf))
            return (scores * decay * step_t[h : h + 1, :]).astype(BF16)

        for q in range(PAIRS):
            lanes = slice(q * PAIR_LANES, (q + 1) * PAIR_LANES)
            x_pair = x_ref[0, :, lanes]
            nothing = jnp.zeros_like(x_pair)
            both = jnp.concatenate([jnp.where(low, x_pair, nothing), jnp.where(low, nothing, x_pair)], axis=0)
            blend = jnp.concatenate([mix(2 * q), mix(2 * q + 1)], axis=1)
            diagonal = jnp.dot(blend, both, preferred_element_type=F32)
            out_ref[0, :, lanes] = diagonal + skip_ref[:, lanes] * x_pair.astype(F32)


def local_part(g, valid, x_in, b_flat, c_flat, cum, cum_t, step_t, skip_lanes):
    requests, span, _ = x_in.shape
    column = pl.BlockSpec((1, 1, span, PER_GROUP), lambda r, v: (r, g, 0, 0))
    as_row = pl.BlockSpec((1, 1, PER_GROUP, span), lambda r, v: (r, g, 0, 0))
    return pl.pallas_call(
        local_body,
        grid_spec=pltpu.PrefetchScalarGridSpec(
            num_scalar_prefetch=1,
            grid=(requests,),
            in_specs=[
                pl.BlockSpec((1, span, GROUP_LANES), lambda r, v: (r, 0, g)),
                pl.BlockSpec((1, span, STATE), lambda r, v: (r, 0, g)),
                pl.BlockSpec((1, span, STATE), lambda r, v: (r, 0, g)),
                column,
                as_row,
                as_row,
                pl.BlockSpec((1, GROUP_LANES), lambda r, v: (0, g)),
            ],
            out_specs=pl.BlockSpec((1, span, GROUP_LANES), lambda r, v: (r, 0, 0)),
        ),
        out_shape=jax.ShapeDtypeStruct((requests, span, GROUP_LANES), F32),
        cost_estimate=cost(1_000_000_000, 10_000_000),
        name="local_part",
    )(valid, x_in, b_flat, c_flat, cum, cum_t, step_t, skip_lanes)


def out_body(
    ahead_of, init_of, unit_lanes, group, part, scalars, local_ref, c_ref, growth_ref, z_ref, gain_ref, before_ref, *refs
):
    n_ahead = len({i for i in ahead_of if i is not None})
    n_init = len({i for i in init_of if i is not None})
    ahead_refs, init_refs = refs[:n_ahead], refs[n_ahead : n_ahead + n_init]
    out_ref, ahead_buf, init_buf, sems = refs[-4:]
    me = scalars[0]
    i = pl.program_id(0)
    span = local_ref.shape[1]

    @pl.when(i == 0)
    def _():
        for device in range(len(ahead_of)):

            @pl.when(me == device)
            def _(device=device):
                copies = []
                if ahead_of[device] is None:
                    ahead_buf[...] = jnp.zeros_like(ahead_buf)
                else:
                    copies.append(pltpu.make_async_copy(ahead_refs[ahead_of[device]], ahead_buf, sems.at[0]))
                if init_of[device] is None:
                    init_buf[...] = jnp.zeros_like(init_buf)
                else:
                    source = init_refs[init_of[device]].at[pl.ds(part * REQ_CHUNK, REQ_CHUNK)]
                    copies.append(pltpu.make_async_copy(source, init_buf, sems.at[1]))
                for copy in copies:
                    copy.start()
                for copy in copies:
                    copy.wait()

    valid = scalars[1 + part * REQ_CHUNK + i]

    @pl.when(valid == 0)
    def _():
        out_ref[...] = jnp.zeros_like(out_ref)

    @pl.when(valid > 0)
    def _():
        low = low_half(span)
        started = before_ref[0] * init_buf[i].astype(F32)
        lane = lax.broadcasted_iota(jnp.int32, (1, GROUP_LANES), 1) + group * GROUP_LANES
        started = jnp.where(lane >= me * unit_lanes, started, 0.0)
        state = (ahead_buf[i].astype(F32) + started).astype(BF16)
        carried = jnp.dot(c_ref[0], state, preferred_element_type=F32)
        growth = growth_ref[0, 0]
        gated = []
        squares = jnp.zeros((span, PAIR_LANES), F32)
        for q in range(PAIRS):
            lanes = slice(q * PAIR_LANES, (q + 1) * PAIR_LANES)
            summed = local_ref[0, :, lanes] + carried[:, lanes] * spread_pair(growth, q, low)
            gate = z_ref[0, :, lanes].astype(F32)
            value = summed.astype(BF16).astype(F32) * (gate / (1.0 + jnp.exp(-gate)))
            gated.append(value)
            squares = squares + value * value
        inverse = lax.rsqrt(jnp.sum(squares, axis=1, keepdims=True) * (1.0 / GROUP_LANES) + EPS)
        for q in range(PAIRS):
            lanes = slice(q * PAIR_LANES, (q + 1) * PAIR_LANES)
            out_ref[0, :, lanes] = (gated[q] * inverse * gain_ref[:, lanes]).astype(BF16)


def out_chunk(scalars, group, part, unit_lanes, local, c_flat, growth, z_in, gain, before, ahead_of, ahead, init_of, inits, y_so_far):
    requests, span, width = z_in.shape
    any_spec = pl.BlockSpec(memory_space=pl.ANY)

    def row(i, s):
        return part * REQ_CHUNK + i

    operands = [local, c_flat, growth, z_in, gain, before, *ahead, *inits]
    in_specs = [
        pl.BlockSpec((1, span, GROUP_LANES), lambda i, s: (row(i, s), 0, 0)),
        pl.BlockSpec((1, span, STATE), lambda i, s: (row(i, s), 0, group)),
        pl.BlockSpec((1, 1, span, PER_GROUP), lambda i, s: (row(i, s), group, 0, 0)),
        pl.BlockSpec((1, span, GROUP_LANES), lambda i, s: (row(i, s), 0, group)),
        pl.BlockSpec((1, GROUP_LANES), lambda i, s: (0, group)),
        pl.BlockSpec((1, 1, GROUP_LANES), lambda i, s: (row(i, s), 0, group)),
    ] + [any_spec] * (len(ahead) + len(inits))
    aliases = {}
    if y_so_far is not None:
        aliases = {1 + len(operands): 0}
        operands.append(y_so_far)
        in_specs.append(any_spec)
    buffer = pltpu.VMEM((REQ_CHUNK, STATE, GROUP_LANES), BF16)
    return pl.pallas_call(
        functools.partial(out_body, ahead_of, init_of, unit_lanes, group, part),
        grid_spec=pltpu.PrefetchScalarGridSpec(
            num_scalar_prefetch=1,
            grid=(REQ_CHUNK,),
            in_specs=in_specs,
            out_specs=pl.BlockSpec((1, span, GROUP_LANES), lambda i, s: (row(i, s), 0, group)),
            scratch_shapes=[buffer, buffer, pltpu.SemaphoreType.DMA((2,))],
        ),
        out_shape=jax.ShapeDtypeStruct((requests, span, width), BF16),
        input_output_aliases=aliases,
        cost_estimate=cost(200_000_000, 4_000_000),
        name="out_chunk",
    )(scalars, *operands)


def kept_rows(cache_states):
    holders = lax.axis_size("cache")
    me = lax.axis_index("cache")
    pieces = [lax.dynamic_index_in_dim(cache_states, me, 1, keepdims=False).astype(BF16)]
    for shift in range(1, holders):
        towards = lax.rem(me + shift, holders)
        piece = lax.dynamic_index_in_dim(cache_states, towards, 1, keepdims=False).astype(BF16)
        pairs = [(i, (i + shift) % holders) for i in range(holders)]
        pieces.append(lax.ppermute(piece, "cache", pairs))
    return jnp.concatenate(pieces, axis=0)


def shards(
    x_in, z_in, b_in, c_in, dt_in, dt_bias, a_log, skip_gain, norm_w, cache_states, parent, state_dev, state_slot, spans
):
    me = lax.axis_index("tok")
    toks = lax.axis_size("tok")
    requests, span, width = x_in.shape
    heads_here = dt_in.shape[2]
    groups = width // GROUP_LANES
    parts = requests // REQ_CHUNK
    chunks = groups * parts
    unit = width // toks
    assert span == SPAN and GROUP_LANES % unit == 0

    replica = lax.axis_index("rep")
    parent_here = lax.dynamic_slice_in_dim(parent, replica * requests, requests)
    span_here = lax.dynamic_slice_in_dim(spans, replica * requests, requests)
    valid = (me < span_here).astype(jnp.int32)
    scalars = jnp.concatenate([me.astype(jnp.int32)[None], valid])

    rows = kept_rows(cache_states)
    holders, slots = lax.axis_size("cache"), cache_states.shape[0]
    owner, slot = state_dev[parent_here], state_slot[parent_here]
    place = lax.rem(lax.axis_index("cache") - owner + holders, holders) * slots + slot
    initial = rows[place].reshape(requests, unit, STATE).transpose(0, 2, 1)

    cum, cum_t, step_t, weight, growth, total = prepare(valid, dt_in, dt_bias[None], a_log[None])
    b_flat = b_in.reshape(requests, span, groups * STATE)
    c_flat = c_in.reshape(requests, span, groups * STATE)
    states = block_states(x_in, b_flat, weight)

    totals = lax.all_gather(total[:, 0], "tok")
    order = jnp.arange(toks)[:, None, None]

    def per_lane(exponent):
        return jnp.repeat(jnp.exp(exponent), HEAD_DIM, axis=1)

    def by_chunk(lanes):
        split = lanes.reshape(parts, REQ_CHUNK, groups, GROUP_LANES).transpose(2, 0, 1, 3)
        return jnp.roll(split, -1, axis=0).reshape(chunks, REQ_CHUNK, 1, GROUP_LANES)

    through = by_chunk(per_lane(total[:, 0]))
    before = per_lane(jnp.sum(jnp.where(order < me, totals, 0.0), axis=0))
    before_through = by_chunk(per_lane(jnp.sum(jnp.where(order <= me, totals, 0.0), axis=0)))
    after = by_chunk(per_lane(jnp.sum(jnp.where(order > me, totals, 0.0), axis=0)))

    def unit_slice(by_chunks, which):
        split = by_chunks.reshape(groups, requests, -1, GROUP_LANES)
        lane = which * unit
        place = lax.rem(lane // GROUP_LANES + groups - 1, groups)
        return lax.dynamic_slice(
            split, (place, 0, 0, lax.rem(lane, GROUP_LANES)), (1, requests, split.shape[2], unit)
        )[0]

    own = initial
    if unit < GROUP_LANES:
        blank = jnp.zeros((requests, STATE, GROUP_LANES), BF16)
        own = lax.dynamic_update_slice(blank, initial, (0, 0, lax.rem(me * unit, GROUP_LANES)))
    own = own.reshape(parts, REQ_CHUNK, STATE, GROUP_LANES)
    own_group = (me * unit) // GROUP_LANES

    def pick(values, c):
        return lax.dynamic_index_in_dim(values, c, 0, keepdims=False)

    received, passed = {}, {}

    def pass_on(h):
        if h in passed:
            return passed[h]
        early = h < HOP and (toks > 1) and (h // parts + 1) % groups != 0
        if early:
            passed[h] = states[h]
            return passed[h]
        c = jnp.clip(h - HOP * me, 0, chunks - 1)
        group = lax.rem(c // parts + 1, groups)
        value = pick(states, c).astype(F32)
        if h - HOP in received:
            value = value + pick(through, c) * received[h - HOP].astype(F32)
        mine = pick(before_through, c) * pick(own, lax.rem(c, parts)).astype(F32)
        value = value + jnp.where(group == own_group, mine, 0.0)
        passed[h] = value.astype(BF16)
        return passed[h]

    for h in range(chunks + HOP * (toks - 2)):
        pairs = [(k, k + 1) for k in range(toks - 1) if 0 <= h - HOP * k < chunks]
        received[h] = lax.ppermute(pass_on(h), "tok", pairs)

    backward = [(k, k - 1) for k in range(1, toks)]
    arrived = []
    sent = initial
    for s in range(toks):
        if s:
            which = jnp.clip(s - toks + me, 0, toks - 1)
            later = unit_slice(after, which) * unit_slice(states, which).astype(F32) + arrived[-1].astype(F32)
            sent = jnp.where(s >= toks - me, later.astype(BF16), arrived[-1])
        arrived.append(lax.ppermute(sent, "tok", backward))

    inits = [initial] + arrived[: toks - 1]
    if unit < GROUP_LANES:
        stacked = jnp.stack(inits)[lax.rem(jnp.arange(toks) - me + toks, toks)]
        inits = [stacked.transpose(1, 2, 0, 3).reshape(requests, STATE, width)]

    ends = []
    for part in range(parts):
        value = None
        for device in range(toks):
            chunk = ((device * unit // GROUP_LANES + groups - 1) % groups) * parts + part
            candidate = pass_on(chunk + HOP * device)
            value = candidate if value is None else jnp.where(me == device, candidate, value)
        ends.append(value)
    ends = jnp.concatenate(ends, axis=0)
    if unit < GROUP_LANES:
        ends = lax.dynamic_slice_in_dim(ends, lax.rem(me * unit, GROUP_LANES), unit, 2)
    final = unit_slice(after, me) * ends.astype(F32) + arrived[-1].astype(F32)
    final_state = final.transpose(0, 2, 1).reshape(requests, unit // HEAD_DIM, HEAD_DIM, STATE)

    skip_lanes = jnp.repeat(skip_gain, HEAD_DIM)[None]
    local = {}
    y_out = None
    for j in range(chunks):
        group, part = (j // parts + 1) % groups, j % parts
        if group not in local:
            local[group] = local_part(group, valid, x_in, b_flat, c_flat, cum, cum_t, step_t, skip_lanes)
        ahead_of = [None] + list(range(toks - 1))
        ahead = [received[j + HOP * k] for k in range(toks - 1)]
        if unit < GROUP_LANES:
            init_of, these = [0] * toks, inits
        else:
            holder = group * GROUP_LANES // unit
            init_of = [holder - k if k <= holder else None for k in range(toks)]
            these = inits[: holder + 1]
        y_out = out_chunk(
            scalars, group, part, unit, local[group], c_flat, growth, z_in, norm_w[None], before[:, None],
            ahead_of, ahead, init_of, these, y_out,
        )
    return (y_out, final_state)


def solution(mesh):
    placed = (
        P(("groups", "rep"), "tok", "cache"),
        P(("groups", "rep"), "tok", "cache"),
        P(("groups", "rep"), "tok", "cache", None),
        P(("groups", "rep"), "tok", "cache", None),
        P(("groups", "rep"), "tok", "cache"),
        P("cache"),
        P("cache"),
        P("cache"),
        P("cache"),
        P(("groups", "cache"), None, "tok", None, None),
        P("groups"),
        P("groups"),
        P("groups"),
        P("groups"),
    )
    return jax.shard_map(
        shards,
        mesh=mesh,
        in_specs=placed,
        out_specs=(
            P(("groups", "rep"), "tok", "cache"),
            P(("groups", "rep"), ("cache", "tok"), None, None),
        ),
        check_vma=False,
    )
```

```python
import functools

import jax
import jax.numpy as jnp
from jax import lax
from jax.experimental import pallas as pl
from jax.experimental.pallas import tpu as pltpu
from jax.sharding import PartitionSpec as P

HEADS = 128
HEAD_DIM = 64
GROUPS = 8
STATE = 128
SPAN = 128
EPS = 1e-05

PER_GROUP = HEADS // GROUPS
GROUP_LANES = PER_GROUP * HEAD_DIM
PAIR_LANES = 2 * HEAD_DIM
PAIRS = PER_GROUP // 2
REQ_CHUNK = 2
HOP = 2
THROUGH, BEFORE, BEFORE_THROUGH, AFTER = range(4)

F32 = jnp.float32
BF16 = jnp.bfloat16
VMEM = pltpu.VMEM
SMEM = pltpu.SMEM


def pin(array):
    return pltpu.with_memory_space_constraint(array, VMEM)


def in_hbm(array):
    return pltpu.with_memory_space_constraint(array, pltpu.HBM)


def call(body, outs, ins, *, scalars=(), after=(), name, flops=1_000, nbytes=1_000, scratch=(), limit=12):
    n_scalars, n_ins, n_after = len(scalars), len(ins), len(after)

    def kernel(*refs):
        head = refs[: n_scalars + n_ins]
        body(*head, *refs[n_scalars + n_ins + n_after :])

    space = [pl.BlockSpec(memory_space=SMEM)] * n_scalars + [pl.BlockSpec(memory_space=VMEM)] * (n_ins + n_after)
    pinned = [pin(a) for a in (*ins, *after)]
    single = isinstance(outs[0][0], int)
    outs = (outs,) if single else tuple(outs)
    result = pl.pallas_call(
        kernel,
        out_shape=tuple(VMEM(shape, dtype) for shape, dtype in outs),
        in_specs=space,
        out_specs=(pl.BlockSpec(memory_space=VMEM),) * len(outs),
        scratch_shapes=list(scratch),
        compiler_params=pltpu.CompilerParams(vmem_limit_bytes=limit << 20),
        cost_estimate=pl.CostEstimate(flops=flops, bytes_accessed=nbytes, transcendentals=0),
        name=name,
    )(*scalars, *pinned)
    return result[0] if single else result


def low_half(rows):
    return lax.broadcasted_iota(jnp.int32, (rows, PAIR_LANES), 1) < HEAD_DIM


def spread_pair(values, q, low):
    return jnp.where(low, values[:, 2 * q : 2 * q + 1], values[:, 2 * q + 1 : 2 * q + 2])


def pair_lanes(q):
    return slice(q * PAIR_LANES, (q + 1) * PAIR_LANES)


def on_device(me, count, branch):
    for device in range(count):
        pl.when(me == device)(functools.partial(branch, device))


def softplus(raw):
    return jnp.maximum(raw, 0.0) + jnp.log1p(jnp.exp(-jnp.abs(raw)))


def front_body(
    order, ids, b_ref, c_ref, spans_hbm, dt_hbm, bias_hbm, alog_hbm, skip_hbm, gain_hbm, x_hbm, info, cum_ref, cum_t_ref,
    step_t_ref, weight_ref, growth_ref, x_ref, bias_ref, alog_ref, skip_ref, gain_ref, *rest
):
    outs, (dt_ref, spans, small_sems, x_sems) = rest[:-4], rest[-4:]
    requests, heads_here, span = dt_ref.shape
    pairs = (
        (spans_hbm, spans), (dt_hbm, dt_ref), (bias_hbm, bias_ref), (alog_hbm, alog_ref), (skip_hbm, skip_ref),
        (gain_hbm, gain_ref),
    )
    small = [pltpu.make_async_copy(source, target, small_sems.at[i]) for i, (source, target) in enumerate(pairs)]
    large = []
    for i, group in enumerate(order):
        lanes = pl.ds(group * GROUP_LANES, GROUP_LANES)
        large.append(pltpu.make_async_copy(x_hbm.at[:, :, lanes], x_ref.at[:, :, lanes], x_sems.at[i]))
    for copy in small + large:
        copy.start()
    for i in range(3):
        info[i] = ids[i]
    for copy in small:
        copy.wait()
    rows = lax.broadcasted_iota(jnp.int32, (span, span), 0)
    cols = lax.broadcasted_iota(jnp.int32, (span, span), 1)
    lower = (rows >= cols).astype(F32)
    rate = -jnp.exp(alog_ref[...])
    for r in range(requests):
        blocks = spans[ids[1] * requests + r]
        live = (ids[0] < blocks).astype(jnp.int32)
        info[3 + r] = live
        info[3 + requests + r] = blocks
        step = softplus(dt_ref[r].astype(F32).T + bias_ref[...]) * live.astype(F32)
        cum = jnp.dot(lower, rate * step, precision=lax.Precision.HIGHEST, preferred_element_type=F32)
        weight = jnp.exp(cum[span - 1 : span, :] - cum) * step
        growth = jnp.exp(cum)
        cum_t = cum.T
        step_t = step.T
        for g in range(heads_here // PER_GROUP):
            here = slice(g * PER_GROUP, (g + 1) * PER_GROUP)
            cum_ref[r, g] = cum[:, here]
            weight_ref[r, g] = weight[:, here]
            growth_ref[r, g] = growth[:, here]
            cum_t_ref[r, g] = cum_t[here, :]
            step_t_ref[r, g] = step_t[here, :]
    large[0].wait()
    block_body(order[0], x_ref, b_ref, weight_ref, *outs)
    for copy in large[1:]:
        copy.wait()


def decay_body(info, dt_ref, bias_ref, alog_ref, out_ref):
    requests = out_ref.shape[1]
    heads_here = dt_ref.shape[1]
    toks = dt_ref.shape[0] // requests
    width = out_ref.shape[-1]
    me = info[0]
    rate = -jnp.exp(alog_ref[...])

    def add(n, sums):
        t = me ^ n
        totals = []
        for r in range(requests):
            step = softplus(dt_ref[n * requests + r].astype(F32).T + bias_ref[...])
            live = (t < info[3 + requests + r]).astype(F32)
            totals.append(jnp.sum(step, axis=0, keepdims=True) * (rate * live))
        total = jnp.concatenate(totals, axis=0)
        return tuple(
            held + total * chosen.astype(F32) for held, chosen in zip(sums, (me == t, me > t, me < t))
        )

    blank = jnp.zeros((requests, heads_here), F32)
    through, before, after = lax.fori_loop(0, toks, add, (blank, blank, blank))
    factors = jnp.exp(jnp.concatenate([through, before, before + through, after], axis=0))
    owner = lax.broadcasted_iota(jnp.int32, (heads_here, width), 1) // HEAD_DIM
    head = lax.broadcasted_iota(jnp.int32, (heads_here, width), 0)
    lanes = jnp.dot(
        factors, (owner == head).astype(F32), precision=lax.Precision.HIGHEST, preferred_element_type=F32
    )
    for kind in range(4):
        for r in range(requests):
            row = kind * requests + r
            out_ref[kind, r] = lanes[row : row + 1]


def block_body(group, x_ref, b_ref, weight_ref, *outs):
    low = low_half(x_ref.shape[1])
    base = group * GROUP_LANES
    for part, out_ref in enumerate(outs):
        for i in range(REQ_CHUNK):
            r = part * REQ_CHUNK + i
            weight = weight_ref[r, group]
            scaled = []
            for q in range(PAIRS):
                here = slice(base + q * PAIR_LANES, base + (q + 1) * PAIR_LANES)
                scaled.append((x_ref[r, :, here].astype(F32) * spread_pair(weight, q, low)).astype(BF16))
            b_here = b_ref[r, :, group * STATE : (group + 1) * STATE]
            states = lax.dot_general(
                b_here, jnp.concatenate(scaled, axis=1), (((0,), (0,)), ((), ())), preferred_element_type=F32
            )
            out_ref[i] = states.astype(BF16)


def local_body(group, info, x_ref, b_ref, c_ref, cum_ref, cum_t_ref, step_t_ref, skip_ref, z_hbm, out_ref, z_ref, sem):
    requests, span = x_ref.shape[:2]
    z_copy = pltpu.make_async_copy(z_hbm.at[:, :, pl.ds(group * GROUP_LANES, GROUP_LANES)], z_ref, sem)
    z_copy.start()
    base = group * GROUP_LANES

    @pl.loop(0, requests)
    def _(r):
        @pl.when(info[3 + r] > 0)
        def _():
            rows = lax.broadcasted_iota(jnp.int32, (span, span), 0)
            cols = lax.broadcasted_iota(jnp.int32, (span, span), 1)
            causal = rows >= cols
            low = low_half(span)
            state = slice(group * STATE, (group + 1) * STATE)
            scores = lax.dot_general(
                c_ref[r, :, state], b_ref[r, :, state], (((1,), (1,)), ((), ())), preferred_element_type=F32
            )
            cum = cum_ref[r, group]
            cum_t = cum_t_ref[r, group]
            step_t = step_t_ref[r, group]

            def mix(h):
                apart = cum[:, h : h + 1] - cum_t[h : h + 1, :]
                decay = jnp.exp(jnp.where(causal, apart, -jnp.inf))
                return (scores * decay * step_t[h : h + 1, :]).astype(BF16)

            for q in range(PAIRS):
                here = slice(base + q * PAIR_LANES, base + (q + 1) * PAIR_LANES)
                x_pair = x_ref[r, :, here]
                nothing = jnp.zeros_like(x_pair)
                both = jnp.concatenate([jnp.where(low, x_pair, nothing), jnp.where(low, nothing, x_pair)], axis=0)
                blend = jnp.concatenate([mix(2 * q), mix(2 * q + 1)], axis=1)
                diagonal = jnp.dot(blend, both, preferred_element_type=F32)
                first = group * PER_GROUP + 2 * q
                skip = jnp.where(low[:1], skip_ref[:, first : first + 1], skip_ref[:, first + 1 : first + 2])
                out_ref[r, :, pair_lanes(q)] = diagonal + skip * x_pair.astype(F32)

    z_copy.wait()


def parents_body(requests, unit, info, parent, state_dev, state_slot, cache_hbm, *refs):
    pieces, (out_ref, rows, sems) = refs[:-3], refs[-3:]
    holders = len(pieces) + 1
    places = []
    for r in range(requests):
        kept = parent[info[1] * requests + r]
        places.append((lax.rem(info[2] - state_dev[kept] + holders, holders), state_slot[kept]))

    def own(r, do):
        shift, slot = places[r]

        @pl.when(shift == 0)
        def _():
            do(pltpu.make_async_copy(cache_hbm.at[slot, info[2]], rows.at[r], sems.at[r]))

    for r in range(requests):
        own(r, lambda copy: copy.start())
    for r in range(requests):
        shift, slot = places[r]
        for n, piece in enumerate(pieces):

            @pl.when(shift == n + 1)
            def _(r=r, slot=slot, piece=piece):
                out_ref[r] = piece[slot].T

        own(r, lambda copy: copy.wait())

        @pl.when(shift == 0)
        def _(r=r):
            out_ref[r] = rows[r].astype(BF16).T


def chain_lanes(group, device, unit):
    first = device * unit
    if first // GROUP_LANES != group:
        return None
    low = first % GROUP_LANES
    return slice(low, low + unit)


def shards(
    x_in, z_in, b_in, c_in, dt_in, dt_bias, a_log, skip_gain, norm_w, cache_states, parent, state_dev, state_slot, spans
):
    me = lax.axis_index("tok")
    toks = lax.axis_size("tok")
    holders = lax.axis_size("cache")
    requests, span, width = x_in.shape
    heads_here = dt_in.shape[2]
    groups = width // GROUP_LANES
    parts = requests // REQ_CHUNK
    chunks = groups * parts
    unit = width // toks
    order = [(i + 1) % groups for i in range(groups)]
    where = {group: i for i, group in enumerate(order)}
    assert span == SPAN and GROUP_LANES % unit == 0

    ids = jnp.stack([me, lax.axis_index("rep"), lax.axis_index("cache")]).astype(jnp.int32)


    slots_here = cache_states.shape[0]
    pieces = []
    for shift in range(1, holders):
        towards = lax.rem(lax.axis_index("cache") + shift, holders)
        piece = lax.dynamic_index_in_dim(cache_states, towards, 1, keepdims=False).astype(BF16)
        piece = lax.ppermute(piece, "cache", [(i, (i + shift) % holders) for i in range(holders)])
        pieces.append(pin(piece.reshape(slots_here, unit, STATE)))
    dt_t = dt_in.transpose(0, 2, 1)
    all_dt, step = dt_t, 1
    while step < toks:
        other = lax.ppermute(all_dt, "tok", [(k, k ^ step) for k in range(toks)])
        all_dt = jnp.concatenate([all_dt, other], axis=0)
        step *= 2

    b_flat = pin(b_in.reshape(requests, span, groups * STATE))
    c_flat = pin(c_in.reshape(requests, span, groups * STATE))
    columns = VMEM((requests, groups, span, PER_GROUP), F32)
    as_rows = VMEM((requests, groups, PER_GROUP, span), F32)
    chunk_type = ((REQ_CHUNK, STATE, GROUP_LANES), BF16)
    smem_spec, vmem_spec, any_spec, hbm_spec = (
        pl.BlockSpec(memory_space=space) for space in (SMEM, VMEM, pl.ANY, pltpu.HBM)
    )
    info, cum, cum_t, step_t, weight, growth, x_in, bias, rates, skip, gain, *found = pl.pallas_call(
        lambda *refs: front_body(order, *refs[:10], *refs[11:]),
        out_shape=(
            jax.ShapeDtypeStruct((3 + 2 * requests,), jnp.int32),
            columns, as_rows, as_rows, columns, columns, VMEM(x_in.shape, BF16),
            *(VMEM((1, heads_here), F32),) * 3, VMEM((1, width), F32), *(VMEM(*chunk_type),) * parts,
        ),
        in_specs=[smem_spec] + [vmem_spec] * 2 + [hbm_spec] * 7 + [vmem_spec],
        out_specs=(smem_spec,) + (vmem_spec,) * (10 + parts),
        scratch_shapes=[
            VMEM(dt_t.shape, BF16), SMEM(spans.shape, jnp.int32),
            pltpu.SemaphoreType.DMA((6,)), pltpu.SemaphoreType.DMA((groups,)),
        ],
        compiler_params=pltpu.CompilerParams(vmem_limit_bytes=12 << 20),
        cost_estimate=pl.CostEstimate(flops=1_000, bytes_accessed=1_000, transcendentals=0),
        name="front",
    )(
        ids,
        b_flat,
        c_flat,
        *map(in_hbm, (spans, dt_t, dt_bias[None], a_log[None], skip_gain[None], norm_w[None], x_in)),
        pin(all_dt),
    )
    states = {part: found[part] for part in range(parts)}
    previous = found[-1]

    for i in range(1, groups):
        found = call(
            functools.partial(block_body, order[i]),
            (chunk_type,) * parts,
            (x_in, b_flat, weight),
            after=(previous,),
            name="block_states",
        )
        for part in range(parts):
            states[i * parts + part] = found[part]
        previous = found[-1]

    initial = pl.pallas_call(
        lambda *refs: parents_body(requests, unit, *refs[: 5 + len(pieces)], *refs[6 + len(pieces) :]),
        out_shape=VMEM((requests, STATE, unit), BF16),
        in_specs=[smem_spec] * 4 + [hbm_spec] + [vmem_spec] * (len(pieces) + 1),
        out_specs=vmem_spec,
        scratch_shapes=[VMEM((requests, unit, STATE), F32), pltpu.SemaphoreType.DMA((requests,))],
        compiler_params=pltpu.CompilerParams(vmem_limit_bytes=12 << 20),
        cost_estimate=pl.CostEstimate(flops=1_000, bytes_accessed=1_000, transcendentals=0),
        name="parents",
    )(info, parent, state_dev, state_slot, in_hbm(cache_states.reshape(slots_here, holders, unit, STATE)), *pieces, pin(previous))
    decays = call(
        decay_body,
        ((4, requests, 1, width), F32),
        (all_dt, bias, rates),
        scalars=(info,),
        after=(initial,),
        name="decays",
    )

    def decay_of(decays_ref, kind, r, group, lanes=slice(0, GROUP_LANES)):
        return decays_ref[kind, r, :, group * GROUP_LANES + lanes.start : group * GROUP_LANES + lanes.stop]

    received, arrived = {}, []

    def pass_on(h, after):
        devices = [k for k in range(toks - 1) if 0 <= h - HOP * k < chunks]
        if devices == [0] and chain_lanes(order[h // parts], 0, unit) is None:
            return states[h]
        incoming = [received[h - HOP]] if any(devices) else []
        ins = [states[h - HOP * k] for k in devices] + incoming + [decays, initial]

        def body(ids_ref, *refs):
            state_refs, incoming_refs = refs[: len(devices)], refs[len(devices) : -3]
            decays_ref, initial_ref, out_ref = refs[-3:]

            def branch(n, device):
                c = h - HOP * device
                group, part = order[c // parts], c % parts
                lanes = chain_lanes(group, device, unit)
                for i in range(REQ_CHUNK):
                    r = part * REQ_CHUNK + i
                    value = state_refs[n][i].astype(F32)
                    if device:
                        value = value + decay_of(decays_ref, THROUGH, r, group) * incoming_refs[0][i].astype(F32)
                    out_ref[i] = value.astype(BF16)
                    if lanes is not None:
                        mine = decay_of(decays_ref, BEFORE_THROUGH, r, group, lanes) * initial_ref[r].astype(F32)
                        out_ref[i, :, lanes] = (value[:, lanes] + mine).astype(BF16)

            for n, device in enumerate(devices):
                pl.when(ids_ref[0] == device)(functools.partial(branch, n, device))

        return call(body, chunk_type, ins, scalars=(info,), after=after, name="pass_on")

    def send_up(h, after=()):
        sent = pass_on(h, after)
        pairs = [(k, k + 1) for k in range(toks - 1) if 0 <= h - HOP * k < chunks]
        received[h] = lax.ppermute(sent, "tok", pairs)
        return sent

    backward = [(k, k - 1) for k in range(1, toks)]

    def send_down(s, after=()):
        sent = initial
        if s:
            used = sorted(
                {where[(s - toks + k) * unit // GROUP_LANES] for k in range(1, toks) if s - toks + k >= 0}
            )
            wanted = [i * parts + part for i in used for part in range(parts)]

            def body(ids_ref, decays_ref, incoming_ref, *refs):
                state_refs, out_ref = refs[:-1], refs[-1]

                def branch(device):
                    target = s - toks + device
                    if target < 0:
                        out_ref[...] = incoming_ref[...]
                        return
                    first = target * unit
                    group, low = first // GROUP_LANES, first % GROUP_LANES
                    lanes = slice(low, low + unit)
                    for r in range(requests):
                        chunk = wanted.index(where[group] * parts + r // REQ_CHUNK)
                        state = state_refs[chunk][r % REQ_CHUNK, :, lanes].astype(F32)
                        later = decay_of(decays_ref, AFTER, r, group, lanes) * state
                        if device < toks - 1:
                            later = later + incoming_ref[r].astype(F32)
                        out_ref[r] = later.astype(BF16)

                on_device(ids_ref[0], toks, branch)

            sent = call(
                body,
                ((requests, STATE, unit), BF16),
                [decays, arrived[-1]] + [states[c] for c in wanted],
                scalars=(info,),
                after=after,
                name="pass_down",
            )
        arrived.append(lax.ppermute(sent, "tok", backward))
        return sent

    def local_sums(i, after):
        ins = (x_in, b_flat, c_flat, cum, cum_t, step_t, skip)
        n_ins, n_after = len(ins), len(after)
        return pl.pallas_call(
            lambda *refs: local_body(order[i], *refs[: 1 + n_ins], refs[1 + n_ins], *refs[2 + n_ins + n_after :]),
            out_shape=(VMEM((requests, span, GROUP_LANES), F32), VMEM((requests, span, GROUP_LANES), BF16)),
            in_specs=[smem_spec] + [vmem_spec] * n_ins + [hbm_spec] + [vmem_spec] * n_after,
            out_specs=(vmem_spec, vmem_spec),
            scratch_shapes=[pltpu.SemaphoreType.DMA],
            compiler_params=pltpu.CompilerParams(vmem_limit_bytes=12 << 20),
            cost_estimate=pl.CostEstimate(flops=1_000, bytes_accessed=1_000, transcendentals=0),
            name="local_sums",
        )(info, *(pin(a) for a in ins), in_hbm(z_in), *(pin(a) for a in after))

    def init_for(group):
        if unit == GROUP_LANES:
            inits = [initial] + arrived[:group]
            return inits, [group - k if k <= group else None for k in range(toks)]
        stacked = jnp.stack([initial] + arrived[: toks - 1])[lax.rem(jnp.arange(toks) - me + toks, toks)]
        full = stacked.transpose(1, 2, 0, 3).reshape(requests, STATE, width)
        return [full[:, :, group * GROUP_LANES : (group + 1) * GROUP_LANES]], [0] * toks

    def finish(i, these, y_so_far, after):
        group = order[i]
        inits, init_of = init_for(group)
        ahead = [received[i * parts + part + HOP * k] for part in these for k in range(toks - 1)]
        ins = [*local[i], c_flat, growth, gain, decays, *ahead, *inits]
        n_ahead, n_init = len(ahead), len(inits)
        had = y_so_far is not None
        count = len(these) * REQ_CHUNK

        def body(info_ref, *refs):
            local_ref, z_ref, c_ref, growth_ref, gain_ref, decays_ref = refs[:6]
            ahead_refs, init_refs = refs[6 : 6 + n_ahead], refs[6 + n_ahead : 6 + n_ahead + n_init]
            y_ref, token_ref, state_buf, y_buf, sems = refs[-5:]
            token_ref[...] = jnp.zeros_like(token_ref)

            def merge(device):
                for n, part in enumerate(these):
                    for j in range(REQ_CHUNK):
                        r = part * REQ_CHUNK + j
                        value = jnp.zeros((STATE, GROUP_LANES), F32)
                        if device:
                            value = ahead_refs[n * (toks - 1) + device - 1][j].astype(F32)
                        if init_of[device] is not None:
                            started = init_refs[init_of[device]][r].astype(F32) * decay_of(decays_ref, BEFORE, r, group)
                            if unit < GROUP_LANES:
                                lane = lax.broadcasted_iota(jnp.int32, (1, GROUP_LANES), 1) + group * GROUP_LANES
                                started = jnp.where(lane >= device * unit, started, 0.0)
                            value = value + started
                        state_buf[n * REQ_CHUNK + j] = value.astype(BF16)

            on_device(info_ref[0], toks, merge)
            copies = []
            for n in range(count):
                r = these[n // REQ_CHUNK] * REQ_CHUNK + n % REQ_CHUNK
                valid = info_ref[3 + r] > 0

                @pl.when(jnp.logical_not(valid))
                def _(n=n):
                    y_buf[n] = jnp.zeros_like(y_buf[n])

                @pl.when(valid)
                def _(n=n, r=r):
                    low = low_half(span)
                    c_here = c_ref[r, :, group * STATE : (group + 1) * STATE]
                    carried = jnp.dot(c_here, state_buf[n], preferred_element_type=F32)
                    grown = growth_ref[r, group]
                    gated = []
                    squares = jnp.zeros((span, PAIR_LANES), F32)
                    for q in range(PAIRS):
                        here = pair_lanes(q)
                        summed = local_ref[r, :, here] + carried[:, here] * spread_pair(grown, q, low)
                        gate = z_ref[r, :, here].astype(F32)
                        value = summed.astype(BF16).astype(F32) * (gate / (1.0 + jnp.exp(-gate)))
                        gated.append(value)
                        squares = squares + value * value
                    inverse = lax.rsqrt(jnp.sum(squares, axis=1, keepdims=True) * (1.0 / GROUP_LANES) + EPS)
                    for q in range(PAIRS):
                        gain = gain_ref[:, group * GROUP_LANES + q * PAIR_LANES : group * GROUP_LANES + (q + 1) * PAIR_LANES]
                        y_buf[n, :, pair_lanes(q)] = (gated[q] * inverse * gain).astype(BF16)

                copy = pltpu.make_async_copy(
                    y_buf.at[n],
                    y_ref.at[r, :, pl.ds(group * GROUP_LANES, GROUP_LANES)],
                    sems.at[n],
                )
                copy.start()
                copies.append(copy)
            for copy in copies:
                copy.wait()

        n_after = len(after)

        def kernel(*refs):
            body(*refs[: 1 + len(ins)], *refs[1 + len(ins) + n_after + had :])

        pinned = [pin(a) for a in (*ins, *after)]
        return pl.pallas_call(
            kernel,
            out_shape=(jax.ShapeDtypeStruct((requests, span, width), BF16), VMEM((8, PAIR_LANES), F32)),
            in_specs=[smem_spec] + [vmem_spec] * len(pinned) + [any_spec] * had,
            out_specs=(any_spec, vmem_spec),
            input_output_aliases={1 + len(pinned): 0} if had else {},
            scratch_shapes=[
                VMEM((count, STATE, GROUP_LANES), BF16),
                VMEM((count, span, GROUP_LANES), BF16),
                pltpu.SemaphoreType.DMA((count,)),
            ],
            compiler_params=pltpu.CompilerParams(vmem_limit_bytes=12 << 20),
            cost_estimate=pl.CostEstimate(flops=1_000, bytes_accessed=1_000, transcendentals=0),
            name="finish",
        )(info, *pinned, *([y_so_far] if had else []))

    def final_states(after):
        ahead = {}
        for k in range(1, toks):
            i = where[k * unit // GROUP_LANES]
            for part in range(parts):
                ahead[k, part] = received[i * parts + part + HOP * (k - 1)]
        keys = list(ahead)
        ins = [decays, initial, arrived[-1], *ahead.values(), *(states[c] for c in range(chunks))]
        n_after = len(after)

        def kernel(ids_ref, *refs):
            decays_ref, initial_ref, later_ref = refs[:3]
            ahead_refs = dict(zip(keys, refs[3 : 3 + len(keys)]))
            state_refs = refs[3 + len(keys) : 3 + len(keys) + chunks]
            final_ref, buf, sems = refs[-3:]

            def branch(device):
                first = device * unit
                group, low = first // GROUP_LANES, first % GROUP_LANES
                lanes = slice(low, low + unit)
                for r in range(requests):
                    part, j = r // REQ_CHUNK, r % REQ_CHUNK
                    value = state_refs[where[group] * parts + part][j, :, lanes].astype(F32)
                    value = value + decay_of(decays_ref, BEFORE_THROUGH, r, group, lanes) * initial_ref[r].astype(F32)
                    if device:
                        through = decay_of(decays_ref, THROUGH, r, group, lanes)
                        value = value + through * ahead_refs[device, part][j, :, lanes].astype(F32)
                    value = value * decay_of(decays_ref, AFTER, r, group, lanes)
                    if device < toks - 1:
                        value = value + later_ref[r].astype(F32)
                    buf[r] = value.T

            on_device(ids_ref[0], toks, branch)
            copies = [pltpu.make_async_copy(buf.at[r], final_ref.at[r], sems.at[r]) for r in range(requests)]
            for copy in copies:
                copy.start()
            for copy in copies:
                copy.wait()

        pinned = [pin(a) for a in (*ins, *after)]
        final = pl.pallas_call(
            kernel,
            out_shape=jax.ShapeDtypeStruct((requests, unit, STATE), F32),
            in_specs=[pl.BlockSpec(memory_space=SMEM)] + [pl.BlockSpec(memory_space=VMEM)] * len(pinned),
            out_specs=pl.BlockSpec(memory_space=pl.ANY),
            scratch_shapes=[VMEM((requests, unit, STATE), F32), pltpu.SemaphoreType.DMA((requests,))],
            compiler_params=pltpu.CompilerParams(vmem_limit_bytes=12 << 20),
            cost_estimate=pl.CostEstimate(flops=1_000, bytes_accessed=1_000, transcendentals=0),
            name="final_states",
        )(info, *pinned)
        return final.reshape(requests, unit // HEAD_DIM, HEAD_DIM, STATE)

    slots = chunks + HOP * (toks - 2)
    lag = HOP * (toks - 2) + parts
    for h in range(HOP):
        send_up(h)
    send_down(0)
    local = {0: local_sums(0, (decays,))}
    previous = local[0][0]
    pending = list(range(1, groups))
    downs = list(range(1, toks))
    y_out, done, final = None, 0, None
    for h in range(HOP, slots):
        previous = send_up(h, (previous,))
        if pending:
            i = pending.pop(0)
            local[i] = local_sums(i, (previous,))
            previous = local[i][0]
        elif done < groups - 1 and done * parts + lag + 1 <= h:
            y_out, previous = finish(done, list(range(parts)), y_out, (previous,))
            done += 1
        if downs and h >= round(HOP + 1 + 2.5 * (toks - 1 - len(downs))):
            previous = send_down(downs.pop(0), (previous,))
    for s in downs:
        previous = send_down(s, (previous,))
    while pending:
        i = pending.pop(0)
        local[i] = local_sums(i, (previous,))
        previous = local[i][0]
    while done < groups - 1:
        y_out, previous = finish(done, list(range(parts)), y_out, (previous,))
        done += 1
    for part in range(parts):
        if part == parts - 1:
            final = final_states((previous,))
        y_out, previous = finish(groups - 1, [part], y_out, (previous,))
    return (y_out, final)


def solution(mesh):
    placed = (
        P(("groups", "rep"), "tok", "cache"),
        P(("groups", "rep"), "tok", "cache"),
        P(("groups", "rep"), "tok", "cache", None),
        P(("groups", "rep"), "tok", "cache", None),
        P(("groups", "rep"), "tok", "cache"),
        P("cache"),
        P("cache"),
        P("cache"),
        P("cache"),
        P(("groups", "cache"), None, "tok", None, None),
        P("groups"),
        P("groups"),
        P("groups"),
        P("groups"),
    )
    return jax.shard_map(
        shards,
        mesh=mesh,
        in_specs=placed,
        out_specs=(
            P(("groups", "rep"), "tok", "cache"),
            P(("groups", "rep"), ("cache", "tok"), None, None),
        ),
        check_vma=False,
    )
```

```python
import functools

import jax
import jax.numpy as jnp
from jax import lax
from jax.experimental import pallas as pl
from jax.experimental.pallas import tpu as pltpu
from jax.sharding import PartitionSpec as P

HEADS = 128
HEAD_DIM = 64
GROUPS = 8
STATE = 128
SPAN = 128
EPS = 1e-05

PER_GROUP = HEADS // GROUPS
GROUP_LANES = PER_GROUP * HEAD_DIM
PAIR_LANES = 2 * HEAD_DIM
PAIRS = PER_GROUP // 2
REQ_CHUNK = 2
HOP = 2
THROUGH, BEFORE, BEFORE_THROUGH, AFTER = range(4)

F32 = jnp.float32
BF16 = jnp.bfloat16
VMEM = pltpu.VMEM
SMEM = pltpu.SMEM


def takes(us):
    return pl.CostEstimate(flops=int(us * 4e9), bytes_accessed=int(us * 14e6), transcendentals=0)


def pin(array):
    return pltpu.with_memory_space_constraint(array, VMEM)


def in_hbm(array):
    return pltpu.with_memory_space_constraint(array, pltpu.HBM)


def call(body, outs, ins, *, scalars=(), after=(), name, us=1.0, scratch=(), limit=12):
    n_scalars, n_ins, n_after = len(scalars), len(ins), len(after)

    def kernel(*refs):
        head = refs[: n_scalars + n_ins]
        body(*head, *refs[n_scalars + n_ins + n_after :])

    space = [pl.BlockSpec(memory_space=SMEM)] * n_scalars + [pl.BlockSpec(memory_space=VMEM)] * (n_ins + n_after)
    pinned = [pin(a) for a in (*ins, *after)]
    single = isinstance(outs[0][0], int)
    outs = (outs,) if single else tuple(outs)
    result = pl.pallas_call(
        kernel,
        out_shape=tuple(VMEM(shape, dtype) for shape, dtype in outs),
        in_specs=space,
        out_specs=(pl.BlockSpec(memory_space=VMEM),) * len(outs),
        scratch_shapes=list(scratch),
        compiler_params=pltpu.CompilerParams(vmem_limit_bytes=limit << 20),
        cost_estimate=takes(us),
        name=name,
    )(*scalars, *pinned)
    return result[0] if single else result


def low_half(rows):
    return lax.broadcasted_iota(jnp.int32, (rows, PAIR_LANES), 1) < HEAD_DIM


def spread_pair(values, q, low):
    return jnp.where(low, values[:, 2 * q : 2 * q + 1], values[:, 2 * q + 1 : 2 * q + 2])


def pair_lanes(q):
    return slice(q * PAIR_LANES, (q + 1) * PAIR_LANES)


def on_device(me, count, branch):
    for device in range(count):
        pl.when(me == device)(functools.partial(branch, device))


def softplus(raw):
    return jnp.maximum(raw, 0.0) + jnp.log1p(jnp.exp(-jnp.abs(raw)))


def front_body(
    order, ids, b_ref, c_ref, spans_hbm, dt_hbm, bias_hbm, alog_hbm, skip_hbm, gain_hbm, x_hbm, info, cum_ref, cum_t_ref,
    step_t_ref, weight_ref, growth_ref, x_ref, bias_ref, alog_ref, skip_ref, gain_ref, *rest
):
    outs, (dt_ref, spans, small_sems, x_sem) = rest[:-4], rest[-4:]
    requests, heads_here, span = dt_ref.shape
    pairs = (
        (spans_hbm, spans), (dt_hbm, dt_ref), (bias_hbm, bias_ref), (alog_hbm, alog_ref), (skip_hbm, skip_ref),
        (gain_hbm, gain_ref),
    )
    small = [pltpu.make_async_copy(source, target, small_sems.at[i]) for i, (source, target) in enumerate(pairs)]
    x_copy = pltpu.make_async_copy(x_hbm.at[:, :, pl.ds(order[0] * GROUP_LANES, GROUP_LANES)], x_ref, x_sem)
    for copy in (*small, x_copy):
        copy.start()
    for i in range(3):
        info[i] = ids[i]
    for copy in small:
        copy.wait()
    rows = lax.broadcasted_iota(jnp.int32, (span, span), 0)
    cols = lax.broadcasted_iota(jnp.int32, (span, span), 1)
    lower = (rows >= cols).astype(F32)
    rate = -jnp.exp(alog_ref[...])
    for r in range(requests):
        blocks = spans[ids[1] * requests + r]
        live = (ids[0] < blocks).astype(jnp.int32)
        info[3 + r] = live
        info[3 + requests + r] = blocks
        step = softplus(dt_ref[r].astype(F32).T + bias_ref[...]) * live.astype(F32)
        cum = jnp.dot(lower, rate * step, precision=lax.Precision.HIGHEST, preferred_element_type=F32)
        weight = jnp.exp(cum[span - 1 : span, :] - cum) * step
        growth = jnp.exp(cum)
        cum_t = cum.T
        step_t = step.T
        for g in range(heads_here // PER_GROUP):
            here = slice(g * PER_GROUP, (g + 1) * PER_GROUP)
            cum_ref[r, g] = cum[:, here]
            weight_ref[r, g] = weight[:, here]
            growth_ref[r, g] = growth[:, here]
            cum_t_ref[r, g] = cum_t[here, :]
            step_t_ref[r, g] = step_t[here, :]
    x_copy.wait()
    block_body(order[0], x_ref, b_ref, weight_ref, *outs)


def decay_body(info, *refs):
    dt_refs, (bias_ref, alog_ref, out_ref) = refs[:-3], refs[-3:]
    toks = len(dt_refs)
    requests, heads_here, _ = dt_refs[0].shape
    width = out_ref.shape[-1]
    me = info[0]
    rate = -jnp.exp(alog_ref[...])

    blank = jnp.zeros((requests, heads_here), F32)
    sums = (blank, blank, blank)
    for n, dt_ref in enumerate(dt_refs):
        t = lax.rem(me - n + toks, toks)
        totals = []
        for r in range(requests):
            step = softplus(dt_ref[r].astype(F32).T + bias_ref[...])
            live = (t < info[3 + requests + r]).astype(F32)
            totals.append(jnp.sum(step, axis=0, keepdims=True) * (rate * live))
        total = jnp.concatenate(totals, axis=0)
        sums = [held + total * chosen.astype(F32) for held, chosen in zip(sums, (me == t, me > t, me < t))]
    through, before, after = sums
    factors = jnp.exp(jnp.concatenate([through, before, before + through, after], axis=0))
    owner = lax.broadcasted_iota(jnp.int32, (heads_here, width), 1) // HEAD_DIM
    head = lax.broadcasted_iota(jnp.int32, (heads_here, width), 0)
    lanes = jnp.dot(
        factors, (owner == head).astype(F32), precision=lax.Precision.HIGHEST, preferred_element_type=F32
    )
    for kind in range(4):
        for r in range(requests):
            row = kind * requests + r
            out_ref[kind, r] = lanes[row : row + 1]


def block_body(group, x_ref, b_ref, weight_ref, *outs):
    low = low_half(x_ref.shape[1])
    for part, out_ref in enumerate(outs):
        for i in range(REQ_CHUNK):
            r = part * REQ_CHUNK + i
            weight = weight_ref[r, group]
            scaled = []
            for q in range(PAIRS):
                here = pair_lanes(q)
                scaled.append((x_ref[r, :, here].astype(F32) * spread_pair(weight, q, low)).astype(BF16))
            b_here = b_ref[r, :, group * STATE : (group + 1) * STATE]
            states = lax.dot_general(
                b_here, jnp.concatenate(scaled, axis=1), (((0,), (0,)), ((), ())), preferred_element_type=F32
            )
            out_ref[i] = states.astype(BF16)


def local_body(group, info, x_ref, b_ref, c_ref, cum_ref, cum_t_ref, step_t_ref, skip_ref, z_hbm, out_ref, z_ref, sem):
    requests, span = x_ref.shape[:2]
    z_copy = pltpu.make_async_copy(z_hbm.at[:, :, pl.ds(group * GROUP_LANES, GROUP_LANES)], z_ref, sem)
    z_copy.start()

    @pl.loop(0, requests)
    def _(r):
        @pl.when(info[3 + r] > 0)
        def _():
            rows = lax.broadcasted_iota(jnp.int32, (span, span), 0)
            cols = lax.broadcasted_iota(jnp.int32, (span, span), 1)
            causal = rows >= cols
            low = low_half(span)
            state = slice(group * STATE, (group + 1) * STATE)
            scores = lax.dot_general(
                c_ref[r, :, state], b_ref[r, :, state], (((1,), (1,)), ((), ())), preferred_element_type=F32
            )
            cum = cum_ref[r, group]
            cum_t = cum_t_ref[r, group]
            step_t = step_t_ref[r, group]

            def mix(h):
                apart = cum[:, h : h + 1] - cum_t[h : h + 1, :]
                decay = jnp.exp(jnp.where(causal, apart, -jnp.inf))
                return (scores * decay * step_t[h : h + 1, :]).astype(BF16)

            for q in range(PAIRS):
                here = pair_lanes(q)
                x_pair = x_ref[r, :, here]
                nothing = jnp.zeros_like(x_pair)
                both = jnp.concatenate([jnp.where(low, x_pair, nothing), jnp.where(low, nothing, x_pair)], axis=0)
                blend = jnp.concatenate([mix(2 * q), mix(2 * q + 1)], axis=1)
                diagonal = jnp.dot(blend, both, preferred_element_type=F32)
                first = group * PER_GROUP + 2 * q
                skip = jnp.where(low[:1], skip_ref[:, first : first + 1], skip_ref[:, first + 1 : first + 2])
                out_ref[r, :, pair_lanes(q)] = diagonal + skip * x_pair.astype(F32)

    z_copy.wait()


def parents_body(order, requests, unit, info, parent, state_dev, state_slot, cache_hbm, x_hbm, *refs):
    n_later = len(order) - 1
    pieces, (out_ref, *x_refs), (rows, sems, x_sems) = refs[: -4 - n_later], refs[-4 - n_later : -3], refs[-3:]
    x_copies = [
        pltpu.make_async_copy(x_hbm.at[:, :, pl.ds(group * GROUP_LANES, GROUP_LANES)], x_refs[i], x_sems.at[i])
        for i, group in enumerate(order[1:])
    ]
    holders = len(pieces) + 1
    places = []
    for r in range(requests):
        kept = parent[info[1] * requests + r]
        places.append((lax.rem(info[2] - state_dev[kept] + holders, holders), state_slot[kept]))

    def own(r, do):
        shift, slot = places[r]

        @pl.when(shift == 0)
        def _():
            do(pltpu.make_async_copy(cache_hbm.at[slot, info[2]], rows.at[r], sems.at[r]))

    for r in range(requests):
        own(r, lambda copy: copy.start())
    for copy in x_copies:
        copy.start()
    for r in range(requests):
        shift, slot = places[r]
        for n, piece in enumerate(pieces):

            @pl.when(shift == n + 1)
            def _(r=r, slot=slot, piece=piece):
                out_ref[r] = piece[slot].T

        own(r, lambda copy: copy.wait())

        @pl.when(shift == 0)
        def _(r=r):
            out_ref[r] = rows[r].astype(BF16).T

    for copy in x_copies:
        copy.wait()


def chain_lanes(group, device, unit):
    first = device * unit
    if first // GROUP_LANES != group:
        return None
    low = first % GROUP_LANES
    return slice(low, low + unit)


def shards(
    x_in, z_in, b_in, c_in, dt_in, dt_bias, a_log, skip_gain, norm_w, cache_states, parent, state_dev, state_slot, spans
):
    me = lax.axis_index("tok")
    toks = lax.axis_size("tok")
    holders = lax.axis_size("cache")
    requests, span, width = x_in.shape
    heads_here = dt_in.shape[2]
    groups = width // GROUP_LANES
    parts = requests // REQ_CHUNK
    chunks = groups * parts
    unit = width // toks
    order = [(i + 1) % groups for i in range(groups)]
    where = {group: i for i, group in enumerate(order)}
    assert span == SPAN and GROUP_LANES % unit == 0

    ids = jnp.stack([me, lax.axis_index("rep"), lax.axis_index("cache")]).astype(jnp.int32)


    slots_here = cache_states.shape[0]
    pieces = []
    for shift in range(1, holders):
        towards = lax.rem(lax.axis_index("cache") + shift, holders)
        piece = lax.dynamic_index_in_dim(cache_states, towards, 1, keepdims=False).astype(BF16)
        piece = lax.ppermute(piece, "cache", [(i, (i + shift) % holders) for i in range(holders)])
        pieces.append(pin(piece.reshape(slots_here, unit, STATE)))
    dt_t = dt_in.transpose(0, 2, 1)
    all_dt = [dt_t] + [
        lax.ppermute(dt_t, "tok", [(k, (k + shift) % toks) for k in range(toks)]) for shift in range(1, toks)
    ]

    b_flat = pin(b_in.reshape(requests, span, groups * STATE))
    c_flat = pin(c_in.reshape(requests, span, groups * STATE))
    columns = VMEM((requests, groups, span, PER_GROUP), F32)
    as_rows = VMEM((requests, groups, PER_GROUP, span), F32)
    chunk_type = ((REQ_CHUNK, STATE, GROUP_LANES), BF16)
    smem_spec, vmem_spec, any_spec, hbm_spec = (
        pl.BlockSpec(memory_space=space) for space in (SMEM, VMEM, pl.ANY, pltpu.HBM)
    )
    info, cum, cum_t, step_t, weight, growth, x_first, bias, rates, skip, gain, *found = pl.pallas_call(
        lambda *refs: front_body(order, *refs[:10], *refs[9 + toks :]),
        out_shape=(
            jax.ShapeDtypeStruct((3 + 2 * requests,), jnp.int32),
            columns, as_rows, as_rows, columns, columns, VMEM((requests, span, GROUP_LANES), BF16),
            *(VMEM((1, heads_here), F32),) * 3, VMEM((1, width), F32), *(VMEM(*chunk_type),) * parts,
        ),
        in_specs=[smem_spec] + [vmem_spec] * 2 + [hbm_spec] * 7 + [vmem_spec] * (toks - 1),
        out_specs=(smem_spec,) + (vmem_spec,) * (10 + parts),
        scratch_shapes=[
            VMEM(dt_t.shape, BF16), SMEM(spans.shape, jnp.int32),
            pltpu.SemaphoreType.DMA((6,)), pltpu.SemaphoreType.DMA,
        ],
        compiler_params=pltpu.CompilerParams(vmem_limit_bytes=12 << 20),
        cost_estimate=takes(5.0),
        name="front",
    )(
        ids,
        b_flat,
        c_flat,
        *map(in_hbm, (spans, dt_t, dt_bias[None], a_log[None], skip_gain[None], norm_w[None], x_in)),
        *map(pin, all_dt[1:]),
    )
    states = {part: found[part] for part in range(parts)}
    previous = found[-1]

    initial, *x_groups = pl.pallas_call(
        lambda *refs: parents_body(order, requests, unit, *refs[: 6 + len(pieces)], *refs[7 + len(pieces) :]),
        out_shape=(VMEM((requests, STATE, unit), BF16),) + (VMEM(x_first.shape, BF16),) * (groups - 1),
        in_specs=[smem_spec] * 4 + [hbm_spec] * 2 + [vmem_spec] * (len(pieces) + 1),
        out_specs=(vmem_spec,) * groups,
        scratch_shapes=[
            VMEM((requests, unit, STATE), F32), pltpu.SemaphoreType.DMA((requests,)), pltpu.SemaphoreType.DMA((groups,)),
        ],
        compiler_params=pltpu.CompilerParams(vmem_limit_bytes=12 << 20),
        cost_estimate=takes(2.8),
        name="parents",
    )(info, parent, state_dev, state_slot, in_hbm(cache_states.reshape(slots_here, holders, unit, STATE)), in_hbm(x_in),
        *pieces, pin(previous))
    x_groups = [x_first, *x_groups]
    decays = call(
        decay_body,
        ((4, requests, 1, width), F32),
        (*all_dt, bias, rates),
        scalars=(info,),
        after=(initial,),
        name="decays",
        us=1.7,
    )

    previous = decays
    for i in range(1, groups):
        found = call(
            functools.partial(block_body, order[i]),
            (chunk_type,) * parts,
            (x_groups[i], b_flat, weight),
            after=(previous,),
            name="block_states",
            us=1.6,
        )
        for part in range(parts):
            states[i * parts + part] = found[part]
        previous = found[-1]

    def decay_of(decays_ref, kind, r, group, lanes=slice(0, GROUP_LANES)):
        return decays_ref[kind, r, :, group * GROUP_LANES + lanes.start : group * GROUP_LANES + lanes.stop]

    received, arrived = {}, []

    def pass_on(h, after):
        devices = [k for k in range(toks - 1) if 0 <= h - HOP * k < chunks]
        if devices == [0] and chain_lanes(order[h // parts], 0, unit) is None:
            return states[h]
        incoming = [received[h - HOP]] if any(devices) else []
        ins = [states[h - HOP * k] for k in devices] + incoming + [decays, initial]

        def body(ids_ref, *refs):
            state_refs, incoming_refs = refs[: len(devices)], refs[len(devices) : -3]
            decays_ref, initial_ref, out_ref = refs[-3:]

            def branch(n, device):
                c = h - HOP * device
                group, part = order[c // parts], c % parts
                lanes = chain_lanes(group, device, unit)
                for i in range(REQ_CHUNK):
                    r = part * REQ_CHUNK + i
                    value = state_refs[n][i].astype(F32)
                    if device:
                        value = value + decay_of(decays_ref, THROUGH, r, group) * incoming_refs[0][i].astype(F32)
                    out_ref[i] = value.astype(BF16)
                    if lanes is not None:
                        mine = decay_of(decays_ref, BEFORE_THROUGH, r, group, lanes) * initial_ref[r].astype(F32)
                        out_ref[i, :, lanes] = (value[:, lanes] + mine).astype(BF16)

            for n, device in enumerate(devices):
                pl.when(ids_ref[0] == device)(functools.partial(branch, n, device))

        return call(body, chunk_type, ins, scalars=(info,), after=after, name="pass_on", us=0.8)

    def send_up(h, after=()):
        sent = pass_on(h, after)
        pairs = [(k, k + 1) for k in range(toks - 1) if 0 <= h - HOP * k < chunks]
        received[h] = lax.ppermute(sent, "tok", pairs)
        return sent

    backward = [(k, k - 1) for k in range(1, toks)]

    def send_down(s, after=()):
        sent = initial
        if s:
            used = sorted(
                {where[(s - toks + k) * unit // GROUP_LANES] for k in range(1, toks) if s - toks + k >= 0}
            )
            wanted = [i * parts + part for i in used for part in range(parts)]

            def body(ids_ref, decays_ref, incoming_ref, *refs):
                state_refs, out_ref = refs[:-1], refs[-1]

                def branch(device):
                    target = s - toks + device
                    if target < 0:
                        out_ref[...] = incoming_ref[...]
                        return
                    first = target * unit
                    group, low = first // GROUP_LANES, first % GROUP_LANES
                    lanes = slice(low, low + unit)
                    for r in range(requests):
                        chunk = wanted.index(where[group] * parts + r // REQ_CHUNK)
                        state = state_refs[chunk][r % REQ_CHUNK, :, lanes].astype(F32)
                        later = decay_of(decays_ref, AFTER, r, group, lanes) * state
                        if device < toks - 1:
                            later = later + incoming_ref[r].astype(F32)
                        out_ref[r] = later.astype(BF16)

                on_device(ids_ref[0], toks, branch)

            sent = call(
                body,
                ((requests, STATE, unit), BF16),
                [decays, arrived[-1]] + [states[c] for c in wanted],
                scalars=(info,),
                after=after,
                name="pass_down",
                us=0.8,
            )
        arrived.append(lax.ppermute(sent, "tok", backward))
        return sent

    def local_sums(i, after):
        ins = (x_groups[i], b_flat, c_flat, cum, cum_t, step_t, skip)
        n_ins, n_after = len(ins), len(after)
        return pl.pallas_call(
            lambda *refs: local_body(order[i], *refs[: 1 + n_ins], refs[1 + n_ins], *refs[2 + n_ins + n_after :]),
            out_shape=(VMEM((requests, span, GROUP_LANES), F32), VMEM((requests, span, GROUP_LANES), BF16)),
            in_specs=[smem_spec] + [vmem_spec] * n_ins + [hbm_spec] + [vmem_spec] * n_after,
            out_specs=(vmem_spec, vmem_spec),
            scratch_shapes=[pltpu.SemaphoreType.DMA],
            compiler_params=pltpu.CompilerParams(vmem_limit_bytes=12 << 20),
            cost_estimate=takes(3.0),
            name="local_sums",
        )(info, *(pin(a) for a in ins), in_hbm(z_in), *(pin(a) for a in after))

    def init_for(group):
        if unit == GROUP_LANES:
            inits = [initial] + arrived[:group]
            return inits, [group - k if k <= group else None for k in range(toks)]
        stacked = jnp.stack([initial] + arrived[: toks - 1])[lax.rem(jnp.arange(toks) - me + toks, toks)]
        full = stacked.transpose(1, 2, 0, 3).reshape(requests, STATE, width)
        return [full[:, :, group * GROUP_LANES : (group + 1) * GROUP_LANES]], [0] * toks

    def finish(i, these, y_so_far, after):
        group = order[i]
        inits, init_of = init_for(group)
        ahead = [received[i * parts + part + HOP * k] for part in these for k in range(toks - 1)]
        ins = [*local[i], c_flat, growth, gain, decays, *ahead, *inits]
        n_ahead, n_init = len(ahead), len(inits)
        had = y_so_far is not None
        count = len(these) * REQ_CHUNK

        def body(info_ref, *refs):
            local_ref, z_ref, c_ref, growth_ref, gain_ref, decays_ref = refs[:6]
            ahead_refs, init_refs = refs[6 : 6 + n_ahead], refs[6 + n_ahead : 6 + n_ahead + n_init]
            y_ref, token_ref, state_buf, y_buf, sems = refs[-5:]
            token_ref[...] = jnp.zeros_like(token_ref)

            def merge(device):
                for n, part in enumerate(these):
                    for j in range(REQ_CHUNK):
                        r = part * REQ_CHUNK + j
                        value = jnp.zeros((STATE, GROUP_LANES), F32)
                        if device:
                            value = ahead_refs[n * (toks - 1) + device - 1][j].astype(F32)
                        if init_of[device] is not None:
                            started = init_refs[init_of[device]][r].astype(F32) * decay_of(decays_ref, BEFORE, r, group)
                            if unit < GROUP_LANES:
                                lane = lax.broadcasted_iota(jnp.int32, (1, GROUP_LANES), 1) + group * GROUP_LANES
                                started = jnp.where(lane >= device * unit, started, 0.0)
                            value = value + started
                        state_buf[n * REQ_CHUNK + j] = value.astype(BF16)

            on_device(info_ref[0], toks, merge)
            copies = []
            for n in range(count):
                r = these[n // REQ_CHUNK] * REQ_CHUNK + n % REQ_CHUNK
                valid = info_ref[3 + r] > 0

                @pl.when(jnp.logical_not(valid))
                def _(n=n):
                    y_buf[n] = jnp.zeros_like(y_buf[n])

                @pl.when(valid)
                def _(n=n, r=r):
                    low = low_half(span)
                    c_here = c_ref[r, :, group * STATE : (group + 1) * STATE]
                    carried = jnp.dot(c_here, state_buf[n], preferred_element_type=F32)
                    grown = growth_ref[r, group]
                    gated = []
                    squares = jnp.zeros((span, PAIR_LANES), F32)
                    for q in range(PAIRS):
                        here = pair_lanes(q)
                        summed = local_ref[r, :, here] + carried[:, here] * spread_pair(grown, q, low)
                        gate = z_ref[r, :, here].astype(F32)
                        value = summed.astype(BF16).astype(F32) * (gate / (1.0 + jnp.exp(-gate)))
                        gated.append(value)
                        squares = squares + value * value
                    inverse = lax.rsqrt(jnp.sum(squares, axis=1, keepdims=True) * (1.0 / GROUP_LANES) + EPS)
                    for q in range(PAIRS):
                        gain = gain_ref[:, group * GROUP_LANES + q * PAIR_LANES : group * GROUP_LANES + (q + 1) * PAIR_LANES]
                        y_buf[n, :, pair_lanes(q)] = (gated[q] * inverse * gain).astype(BF16)

                copy = pltpu.make_async_copy(
                    y_buf.at[n],
                    y_ref.at[r, :, pl.ds(group * GROUP_LANES, GROUP_LANES)],
                    sems.at[n],
                )
                copy.start()
                copies.append(copy)
            for copy in copies:
                copy.wait()

        n_after = len(after)

        def kernel(*refs):
            body(*refs[: 1 + len(ins)], *refs[1 + len(ins) + n_after + had :])

        pinned = [pin(a) for a in (*ins, *after)]
        return pl.pallas_call(
            kernel,
            out_shape=(jax.ShapeDtypeStruct((requests, span, width), BF16), VMEM((8, PAIR_LANES), F32)),
            in_specs=[smem_spec] + [vmem_spec] * len(pinned) + [any_spec] * had,
            out_specs=(any_spec, vmem_spec),
            input_output_aliases={1 + len(pinned): 0} if had else {},
            scratch_shapes=[
                VMEM((count, STATE, GROUP_LANES), BF16),
                VMEM((count, span, GROUP_LANES), BF16),
                pltpu.SemaphoreType.DMA((count,)),
            ],
            compiler_params=pltpu.CompilerParams(vmem_limit_bytes=12 << 20),
            cost_estimate=takes(4.0),
            name="finish",
        )(info, *pinned, *([y_so_far] if had else []))

    def final_states(after):
        ahead = {}
        for k in range(1, toks):
            i = where[k * unit // GROUP_LANES]
            for part in range(parts):
                ahead[k, part] = received[i * parts + part + HOP * (k - 1)]
        keys = list(ahead)
        ins = [decays, initial, arrived[-1], *ahead.values(), *(states[c] for c in range(chunks))]
        n_after = len(after)

        def kernel(ids_ref, *refs):
            decays_ref, initial_ref, later_ref = refs[:3]
            ahead_refs = dict(zip(keys, refs[3 : 3 + len(keys)]))
            state_refs = refs[3 + len(keys) : 3 + len(keys) + chunks]
            final_ref, buf, sems = refs[-4:][:1] + refs[-2:]
            refs[-3][...] = jnp.zeros_like(refs[-3])

            def branch(device):
                first = device * unit
                group, low = first // GROUP_LANES, first % GROUP_LANES
                lanes = slice(low, low + unit)
                for r in range(requests):
                    part, j = r // REQ_CHUNK, r % REQ_CHUNK
                    value = state_refs[where[group] * parts + part][j, :, lanes].astype(F32)
                    value = value + decay_of(decays_ref, BEFORE_THROUGH, r, group, lanes) * initial_ref[r].astype(F32)
                    if device:
                        through = decay_of(decays_ref, THROUGH, r, group, lanes)
                        value = value + through * ahead_refs[device, part][j, :, lanes].astype(F32)
                    value = value * decay_of(decays_ref, AFTER, r, group, lanes)
                    if device < toks - 1:
                        value = value + later_ref[r].astype(F32)
                    buf[r] = value.T

            on_device(ids_ref[0], toks, branch)
            copies = [pltpu.make_async_copy(buf.at[r], final_ref.at[r], sems.at[r]) for r in range(requests)]
            for copy in copies:
                copy.start()
            for copy in copies:
                copy.wait()

        pinned = [pin(a) for a in (*ins, *after)]
        final, token = pl.pallas_call(
            kernel,
            out_shape=(jax.ShapeDtypeStruct((requests, unit, STATE), F32), VMEM((8, PAIR_LANES), F32)),
            in_specs=[pl.BlockSpec(memory_space=SMEM)] + [pl.BlockSpec(memory_space=VMEM)] * len(pinned),
            out_specs=(any_spec, vmem_spec),
            scratch_shapes=[VMEM((requests, unit, STATE), F32), pltpu.SemaphoreType.DMA((requests,))],
            compiler_params=pltpu.CompilerParams(vmem_limit_bytes=12 << 20),
            cost_estimate=takes(2.7),
            name="final_states",
        )(info, *pinned)
        return final.reshape(requests, unit // HEAD_DIM, HEAD_DIM, STATE), token

    slots = chunks + HOP * (toks - 2)
    lag = HOP * (toks - 2) + parts
    for h in range(HOP):
        send_up(h)
    send_down(0)
    local = {0: local_sums(0, (previous,))}
    previous = local[0][0]
    pending = list(range(1, groups))
    downs = list(range(1, toks))
    y_out, done, final = None, 0, None
    for h in range(HOP, slots):
        previous = send_up(h, (previous,))
        if pending:
            i = pending.pop(0)
            local[i] = local_sums(i, (previous,))
            previous = local[i][0]
        elif done < groups - 1 and done * parts + lag + 1 <= h:
            y_out, previous = finish(done, list(range(parts)), y_out, (previous,))
            done += 1
        if downs and h >= round(HOP + (1 + 2.5 * (toks - 1 - len(downs))) * parts / 2):
            previous = send_down(downs.pop(0), (previous,))
    for s in downs:
        previous = send_down(s, (previous,))
    while pending:
        i = pending.pop(0)
        local[i] = local_sums(i, (previous,))
        previous = local[i][0]
    while done < groups - 1:
        y_out, previous = finish(done, list(range(parts)), y_out, (previous,))
        done += 1
    for part in range(parts):
        if part == parts - 1:
            final, previous = final_states((previous,))
        y_out, previous = finish(groups - 1, [part], y_out, (previous,))
    return (y_out, final)


def solution(mesh):
    placed = (
        P(("groups", "rep"), "tok", "cache"),
        P(("groups", "rep"), "tok", "cache"),
        P(("groups", "rep"), "tok", "cache", None),
        P(("groups", "rep"), "tok", "cache", None),
        P(("groups", "rep"), "tok", "cache"),
        P("cache"),
        P("cache"),
        P("cache"),
        P("cache"),
        P(("groups", "cache"), None, "tok", None, None),
        P("groups"),
        P("groups"),
        P("groups"),
        P("groups"),
    )
    return jax.shard_map(
        shards,
        mesh=mesh,
        in_specs=placed,
        out_specs=(
            P(("groups", "rep"), "tok", "cache"),
            P(("groups", "rep"), ("cache", "tok"), None, None),
        ),
        check_vma=False,
    )
```

```python
import functools

import jax
import jax.numpy as jnp
from jax import lax
from jax.experimental import pallas as pl
from jax.experimental.pallas import tpu as pltpu
from jax.sharding import PartitionSpec as P

HEADS = 128
HEAD_DIM = 64
GROUPS = 8
STATE = 128
SPAN = 128
EPS = 1e-05

PER_GROUP = HEADS // GROUPS
GROUP_LANES = PER_GROUP * HEAD_DIM
PAIR_LANES = 2 * HEAD_DIM
PAIRS = PER_GROUP // 2
REQ_CHUNK = 2
HOP = 2
THROUGH, BEFORE, BEFORE_THROUGH, AFTER = range(4)

F32 = jnp.float32
BF16 = jnp.bfloat16
VMEM = pltpu.VMEM
SMEM = pltpu.SMEM


def takes(us):
    return pl.CostEstimate(flops=int(us * 4e9), bytes_accessed=int(us * 14e6), transcendentals=0)


def pin(array):
    return pltpu.with_memory_space_constraint(array, VMEM)


def in_hbm(array):
    return pltpu.with_memory_space_constraint(array, pltpu.HBM)


def call(body, outs, ins, *, scalars=(), after=(), name, us=1.0, scratch=(), limit=12):
    n_scalars, n_ins, n_after = len(scalars), len(ins), len(after)

    def kernel(*refs):
        head = refs[: n_scalars + n_ins]
        body(*head, *refs[n_scalars + n_ins + n_after :])

    space = [pl.BlockSpec(memory_space=SMEM)] * n_scalars + [pl.BlockSpec(memory_space=VMEM)] * (n_ins + n_after)
    pinned = [pin(a) for a in (*ins, *after)]
    single = isinstance(outs[0][0], int)
    outs = (outs,) if single else tuple(outs)
    result = pl.pallas_call(
        kernel,
        out_shape=tuple(VMEM(shape, dtype) for shape, dtype in outs),
        in_specs=space,
        out_specs=(pl.BlockSpec(memory_space=VMEM),) * len(outs),
        scratch_shapes=list(scratch),
        compiler_params=pltpu.CompilerParams(vmem_limit_bytes=limit << 20),
        cost_estimate=takes(us),
        name=name,
    )(*scalars, *pinned)
    return result[0] if single else result


def low_half(rows):
    return lax.broadcasted_iota(jnp.int32, (rows, PAIR_LANES), 1) < HEAD_DIM


def spread_pair(values, q, low):
    return jnp.where(low, values[:, 2 * q : 2 * q + 1], values[:, 2 * q + 1 : 2 * q + 2])


def pair_lanes(q):
    return slice(q * PAIR_LANES, (q + 1) * PAIR_LANES)


def on_device(me, count, branch):
    for device in range(count):
        pl.when(me == device)(functools.partial(branch, device))


def softplus(raw):
    return jnp.maximum(raw, 0.0) + jnp.log1p(jnp.exp(-jnp.abs(raw)))


def front_body(
    order, ids, spans_hbm, b_hbm, dt_hbm, bias_hbm, alog_hbm, skip_hbm, gain_hbm, x_hbm, info, cum_ref, cum_t_ref,
    step_t_ref, weight_ref, growth_ref, x_ref, b_ref, dt_ref, bias_ref, alog_ref, skip_ref, gain_ref, *rest
):
    outs, (raw_b, spans, small_sems, x_sem) = rest[:-4], rest[-4:]
    requests, heads_here, span = dt_ref.shape
    pairs = (
        (spans_hbm, spans), (dt_hbm, dt_ref), (bias_hbm, bias_ref), (alog_hbm, alog_ref), (skip_hbm, skip_ref),
        (gain_hbm, gain_ref), (b_hbm, raw_b),
    )
    small = [pltpu.make_async_copy(source, target, small_sems.at[i]) for i, (source, target) in enumerate(pairs)]
    x_copy = pltpu.make_async_copy(x_hbm.at[:, :, pl.ds(order[0] * GROUP_LANES, GROUP_LANES)], x_ref, x_sem)
    for copy in (*small, x_copy):
        copy.start()
    for i in range(3):
        info[i] = ids[i]
    for copy in small:
        copy.wait()
    rows = lax.broadcasted_iota(jnp.int32, (span, span), 0)
    cols = lax.broadcasted_iota(jnp.int32, (span, span), 1)
    lower = (rows >= cols).astype(F32)
    rate = -jnp.exp(alog_ref[...])
    for r in range(requests):
        blocks = spans[ids[1] * requests + r]
        live = (ids[0] < blocks).astype(jnp.int32)
        info[3 + r] = live
        info[3 + requests + r] = blocks
        step = softplus(dt_ref[r].astype(F32).T + bias_ref[...]) * live.astype(F32)
        cum = jnp.dot(lower, rate * step, precision=lax.Precision.HIGHEST, preferred_element_type=F32)
        weight = jnp.exp(cum[span - 1 : span, :] - cum) * step
        growth = jnp.exp(cum)
        cum_t = cum.T
        step_t = step.T
        for g in range(heads_here // PER_GROUP):
            here = slice(g * PER_GROUP, (g + 1) * PER_GROUP)
            cum_ref[r, g] = cum[:, here]
            weight_ref[r, g] = weight[:, here]
            growth_ref[r, g] = growth[:, here]
            cum_t_ref[r, g] = cum_t[here, :]
            step_t_ref[r, g] = step_t[here, :]
    for r in range(requests):
        b_ref[r] = raw_b[r].reshape(b_ref.shape[1:])
    x_copy.wait()
    block_body(order[0], x_ref, b_ref, weight_ref, *outs)


def decay_body(info, *refs):
    dt_refs, (bias_ref, alog_ref, out_ref) = refs[:-3], refs[-3:]
    toks = len(dt_refs)
    requests, heads_here, _ = dt_refs[0].shape
    width = out_ref.shape[-1]
    me = info[0]
    rate = -jnp.exp(alog_ref[...])

    blank = jnp.zeros((requests, heads_here), F32)
    sums = (blank, blank, blank)
    for n, dt_ref in enumerate(dt_refs):
        t = lax.rem(me - n + toks, toks)
        totals = []
        for r in range(requests):
            step = softplus(dt_ref[r].astype(F32).T + bias_ref[...])
            live = (t < info[3 + requests + r]).astype(F32)
            totals.append(jnp.sum(step, axis=0, keepdims=True) * (rate * live))
        total = jnp.concatenate(totals, axis=0)
        sums = [held + total * chosen.astype(F32) for held, chosen in zip(sums, (me == t, me > t, me < t))]
    through, before, after = sums
    factors = jnp.exp(jnp.concatenate([through, before, before + through, after], axis=0))
    owner = lax.broadcasted_iota(jnp.int32, (heads_here, width), 1) // HEAD_DIM
    head = lax.broadcasted_iota(jnp.int32, (heads_here, width), 0)
    lanes = jnp.dot(
        factors, (owner == head).astype(F32), precision=lax.Precision.HIGHEST, preferred_element_type=F32
    )
    for kind in range(4):
        for r in range(requests):
            row = kind * requests + r
            out_ref[kind, r] = lanes[row : row + 1]


def block_body(group, x_ref, b_ref, weight_ref, *outs):
    low = low_half(x_ref.shape[1])
    for part, out_ref in enumerate(outs):
        for i in range(REQ_CHUNK):
            r = part * REQ_CHUNK + i
            weight = weight_ref[r, group]
            scaled = []
            for q in range(PAIRS):
                here = pair_lanes(q)
                scaled.append((x_ref[r, :, here].astype(F32) * spread_pair(weight, q, low)).astype(BF16))
            b_here = b_ref[r, :, group * STATE : (group + 1) * STATE]
            states = lax.dot_general(
                b_here, jnp.concatenate(scaled, axis=1), (((0,), (0,)), ((), ())), preferred_element_type=F32
            )
            out_ref[i] = states.astype(BF16)


def local_body(group, info, x_ref, b_ref, c_ref, cum_ref, cum_t_ref, step_t_ref, skip_ref, z_hbm, out_ref, z_ref, sem):
    requests, span = x_ref.shape[:2]
    z_copy = pltpu.make_async_copy(z_hbm.at[:, :, pl.ds(group * GROUP_LANES, GROUP_LANES)], z_ref, sem)
    z_copy.start()

    @pl.loop(0, requests)
    def _(r):
        @pl.when(info[3 + r] > 0)
        def _():
            rows = lax.broadcasted_iota(jnp.int32, (span, span), 0)
            cols = lax.broadcasted_iota(jnp.int32, (span, span), 1)
            causal = rows >= cols
            low = low_half(span)
            state = slice(group * STATE, (group + 1) * STATE)
            scores = lax.dot_general(
                c_ref[r, :, state], b_ref[r, :, state], (((1,), (1,)), ((), ())), preferred_element_type=F32
            )
            cum = cum_ref[r, group]
            cum_t = cum_t_ref[r, group]
            step_t = step_t_ref[r, group]

            def mix(h):
                apart = cum[:, h : h + 1] - cum_t[h : h + 1, :]
                decay = jnp.exp(jnp.where(causal, apart, -jnp.inf))
                return (scores * decay * step_t[h : h + 1, :]).astype(BF16)

            for q in range(PAIRS):
                here = pair_lanes(q)
                x_pair = x_ref[r, :, here]
                nothing = jnp.zeros_like(x_pair)
                both = jnp.concatenate([jnp.where(low, x_pair, nothing), jnp.where(low, nothing, x_pair)], axis=0)
                blend = jnp.concatenate([mix(2 * q), mix(2 * q + 1)], axis=1)
                diagonal = jnp.dot(blend, both, preferred_element_type=F32)
                first = group * PER_GROUP + 2 * q
                skip = jnp.where(low[:1], skip_ref[:, first : first + 1], skip_ref[:, first + 1 : first + 2])
                out_ref[r, :, pair_lanes(q)] = diagonal + skip * x_pair.astype(F32)

    z_copy.wait()


def parents_body(requests, info, parent, state_dev, state_slot, cache_hbm, *refs):
    pieces, (out_ref, rows, sems) = refs[:-3], refs[-3:]
    holders = len(pieces) + 1
    places = []
    for r in range(requests):
        kept = parent[info[1] * requests + r]
        places.append((lax.rem(info[2] - state_dev[kept] + holders, holders), state_slot[kept]))

    def own(r, do):
        shift, slot = places[r]

        @pl.when(shift == 0)
        def _():
            do(pltpu.make_async_copy(cache_hbm.at[slot, info[2]], rows.at[r], sems.at[r]))

    for r in range(requests):
        own(r, lambda copy: copy.start())
    for r in range(requests):
        shift, slot = places[r]
        for n, piece in enumerate(pieces):

            @pl.when(shift == n + 1)
            def _(r=r, slot=slot, piece=piece):
                out_ref[r] = piece[slot].T

        own(r, lambda copy: copy.wait())

        @pl.when(shift == 0)
        def _(r=r):
            out_ref[r] = rows[r].astype(BF16).T


def chain_lanes(group, device, unit):
    first = device * unit
    if first // GROUP_LANES != group:
        return None
    low = first % GROUP_LANES
    return slice(low, low + unit)


def shards(
    x_in, z_in, b_in, c_in, dt_in, dt_bias, a_log, skip_gain, norm_w, cache_states, parent, state_dev, state_slot, spans
):
    me = lax.axis_index("tok")
    toks = lax.axis_size("tok")
    holders = lax.axis_size("cache")
    requests, span, width = x_in.shape
    heads_here = dt_in.shape[2]
    groups = width // GROUP_LANES
    parts = requests // REQ_CHUNK
    chunks = groups * parts
    unit = width // toks
    order = [(i + 2) % groups for i in range(groups)]
    where = {group: i for i, group in enumerate(order)}
    assert span == SPAN and GROUP_LANES % unit == 0

    ids = jnp.stack([me, lax.axis_index("rep"), lax.axis_index("cache")]).astype(jnp.int32)


    dt_t = dt_in.transpose(0, 2, 1)
    flat = VMEM((requests, span, groups * STATE), BF16)
    columns = VMEM((requests, groups, span, PER_GROUP), F32)
    as_rows = VMEM((requests, groups, PER_GROUP, span), F32)
    chunk_type = ((REQ_CHUNK, STATE, GROUP_LANES), BF16)
    smem_spec, vmem_spec, any_spec, hbm_spec = (
        pl.BlockSpec(memory_space=space) for space in (SMEM, VMEM, pl.ANY, pltpu.HBM)
    )
    info, cum, cum_t, step_t, weight, growth, x_first, b_flat, dt_here, bias, rates, skip, gain, *found = pl.pallas_call(
        functools.partial(front_body, order),
        out_shape=(
            jax.ShapeDtypeStruct((3 + 2 * requests,), jnp.int32),
            columns, as_rows, as_rows, columns, columns, VMEM((requests, span, GROUP_LANES), BF16), flat, VMEM(dt_t.shape, BF16),
            *(VMEM((1, heads_here), F32),) * 3, VMEM((1, width), F32), *(VMEM(*chunk_type),) * parts,
        ),
        in_specs=[smem_spec] + [hbm_spec] * 8,
        out_specs=(smem_spec,) + (vmem_spec,) * (12 + parts),
        scratch_shapes=[
            VMEM(b_in.shape, BF16), SMEM(spans.shape, jnp.int32),
            pltpu.SemaphoreType.DMA((7,)), pltpu.SemaphoreType.DMA,
        ],
        compiler_params=pltpu.CompilerParams(vmem_limit_bytes=12 << 20),
        cost_estimate=takes(5.0),
        name="front",
    )(
        ids,
        *map(in_hbm, (spans, b_in, dt_t, dt_bias[None], a_log[None], skip_gain[None], norm_w[None], x_in)),
    )
    states = {part: found[part] for part in range(parts)}
    previous = found[-1]

    slots_here = cache_states.shape[0]
    cache_rows = in_hbm(cache_states.reshape(slots_here, holders, unit, STATE))

    def load_body(info_ref, cache_hbm, x_hbm, c_hbm, _, *refs):
        piece_refs, c_ref, x_refs = refs[: holders - 1], refs[holders - 1], refs[holders : holders + groups - 1]
        rows_ref, raw_c, sems = refs[-3:]
        copies = []
        for n in range(holders - 1):
            towards = lax.rem(info_ref[2] + n + 1, holders)
            copies.append(pltpu.make_async_copy(cache_hbm.at[:, towards], rows_ref.at[n], sems.at[n]))
        copies.append(pltpu.make_async_copy(c_hbm, raw_c, sems.at[holders - 1]))
        for n, group in enumerate(order[1:]):
            lanes = pl.ds(group * GROUP_LANES, GROUP_LANES)
            copies.append(pltpu.make_async_copy(x_hbm.at[:, :, lanes], x_refs[n], sems.at[holders + n]))
        for copy in copies:
            copy.start()
        for n in range(holders - 1):
            copies[n].wait()
            piece_refs[n][...] = rows_ref[n].astype(BF16)
        copies[holders - 1].wait()
        for r in range(requests):
            c_ref[r] = raw_c[r].reshape(c_ref.shape[1:])
        for copy in copies[holders:]:
            copy.wait()

    piece_type = (slots_here, unit, STATE)
    loaded = pl.pallas_call(
        load_body,
        out_shape=(VMEM(piece_type, BF16),) * (holders - 1) + (flat,) + (VMEM(x_first.shape, BF16),) * (groups - 1),
        in_specs=[smem_spec] + [hbm_spec] * 3 + [vmem_spec],
        out_specs=(vmem_spec,) * (holders + groups - 1),
        scratch_shapes=[
            VMEM((holders - 1, *piece_type), F32), VMEM(c_in.shape, BF16), pltpu.SemaphoreType.DMA((holders + groups,)),
        ],
        compiler_params=pltpu.CompilerParams(vmem_limit_bytes=12 << 20),
        cost_estimate=takes(3.0),
        name="loads",
    )(info, cache_rows, in_hbm(x_in), in_hbm(c_in), pin(previous))
    all_dt = [dt_here] + [
        lax.ppermute(dt_here, "tok", [(k, (k + shift) % toks) for k in range(toks)]) for shift in range(1, toks)
    ]
    pieces = [
        pin(lax.ppermute(loaded[n], "cache", [(i, (i + n + 1) % holders) for i in range(holders)]))
        for n in range(holders - 1)
    ]
    c_flat, x_groups = loaded[holders - 1], [x_first, *loaded[holders:]]
    def find_states(i, after):
        found = call(
            functools.partial(block_body, order[i]),
            (chunk_type,) * parts,
            (x_groups[i], b_flat, weight),
            after=after,
            name="block_states",
            us=0.4,
        )
        for part in range(parts):
            states[i * parts + part] = found[part]
        return found[-1]

    def decay_of(decays_ref, kind, r, group, lanes=slice(0, GROUP_LANES)):
        return decays_ref[kind, r, :, group * GROUP_LANES + lanes.start : group * GROUP_LANES + lanes.stop]

    received, arrived = {}, []

    def pass_on(h, after):
        devices = [k for k in range(toks - 1) if 0 <= h - HOP * k < chunks]
        if devices == [0] and chain_lanes(order[h // parts], 0, unit) is None:
            return states[h]
        incoming = [received[h - HOP]] if any(devices) else []
        merging = any(chain_lanes(order[(h - HOP * k) // parts], k, unit) is not None for k in devices)
        ins = [states[h - HOP * k] for k in devices] + incoming + [growth] + (started[::-1] if merging else [])

        def body(ids_ref, *refs):
            out_ref = refs[-1]
            state_refs, refs = refs[: len(devices)], refs[len(devices) : -1]
            incoming_ref, refs = (refs[0], refs[1:]) if incoming else (None, refs)
            growth_ref = refs[0]

            def branch(n, device):
                c = h - HOP * device
                group, part = order[c // parts], c % parts
                lanes = chain_lanes(group, device, unit)
                low = low_half(1)
                for i in range(REQ_CHUNK):
                    r = part * REQ_CHUNK + i
                    value = state_refs[n][i].astype(F32)
                    if device:
                        through = growth_ref[r, group, span - 1 : span, :]
                        through = jnp.concatenate([spread_pair(through, q, low) for q in range(PAIRS)], axis=1)
                        value = value + through * incoming_ref[i].astype(F32)
                    out_ref[i] = value.astype(BF16)
                    if lanes is not None:
                        decays_ref, initial_ref = refs[1:]
                        mine = decay_of(decays_ref, BEFORE_THROUGH, r, group, lanes) * initial_ref[r].astype(F32)
                        out_ref[i, :, lanes] = (value[:, lanes] + mine).astype(BF16)

            for n, device in enumerate(devices):
                pl.when(ids_ref[0] == device)(functools.partial(branch, n, device))

        return call(body, chunk_type, ins, scalars=(info,), after=after, name="pass_on", us=0.8)

    def send_up(h, after=()):
        sent = pass_on(h, after)
        pairs = [(k, k + 1) for k in range(toks - 1) if 0 <= h - HOP * k < chunks]
        received[h] = lax.ppermute(sent, "tok", pairs)
        return sent

    backward = [(k, k - 1) for k in range(1, toks)]

    def send_down(s, after=()):
        initial, decays = started
        sent = initial
        if s:
            used = sorted(
                {where[(s - toks + k) * unit // GROUP_LANES] for k in range(1, toks) if s - toks + k >= 0}
            )
            wanted = [i * parts + part for i in used for part in range(parts)]

            def body(ids_ref, decays_ref, incoming_ref, *refs):
                state_refs, out_ref = refs[:-1], refs[-1]

                def branch(device):
                    target = s - toks + device
                    if target < 0:
                        out_ref[...] = incoming_ref[...]
                        return
                    first = target * unit
                    group, low = first // GROUP_LANES, first % GROUP_LANES
                    lanes = slice(low, low + unit)
                    for r in range(requests):
                        chunk = wanted.index(where[group] * parts + r // REQ_CHUNK)
                        state = state_refs[chunk][r % REQ_CHUNK, :, lanes].astype(F32)
                        later = decay_of(decays_ref, AFTER, r, group, lanes) * state
                        if device < toks - 1:
                            later = later + incoming_ref[r].astype(F32)
                        out_ref[r] = later.astype(BF16)

                on_device(ids_ref[0], toks, branch)

            sent = call(
                body,
                ((requests, STATE, unit), BF16),
                [decays, arrived[-1]] + [states[c] for c in wanted],
                scalars=(info,),
                after=after,
                name="pass_down",
                us=0.8,
            )
        arrived.append(lax.ppermute(sent, "tok", backward))
        return sent

    def local_sums(i, after):
        ins = (x_groups[i], b_flat, c_flat, cum, cum_t, step_t, skip)
        n_ins, n_after = len(ins), len(after)
        return pl.pallas_call(
            lambda *refs: local_body(order[i], *refs[: 1 + n_ins], refs[1 + n_ins], *refs[2 + n_ins + n_after :]),
            out_shape=(VMEM((requests, span, GROUP_LANES), F32), VMEM((requests, span, GROUP_LANES), BF16)),
            in_specs=[smem_spec] + [vmem_spec] * n_ins + [hbm_spec] + [vmem_spec] * n_after,
            out_specs=(vmem_spec, vmem_spec),
            scratch_shapes=[pltpu.SemaphoreType.DMA],
            compiler_params=pltpu.CompilerParams(vmem_limit_bytes=12 << 20),
            cost_estimate=takes(3.0),
            name="local_sums",
        )(info, *(pin(a) for a in ins), in_hbm(z_in), *(pin(a) for a in after))

    def init_for(group):
        initial = started[0]
        if unit == GROUP_LANES:
            inits = [initial] + arrived[:group]
            return inits, [group - k if k <= group else None for k in range(toks)]
        stacked = jnp.stack([initial] + arrived[: toks - 1])[lax.rem(jnp.arange(toks) - me + toks, toks)]
        full = stacked.transpose(1, 2, 0, 3).reshape(requests, STATE, width)
        return [full[:, :, group * GROUP_LANES : (group + 1) * GROUP_LANES]], [0] * toks

    def finish(i, these, y_so_far, after):
        group = order[i]
        inits, init_of = init_for(group)
        decays = started[1]
        ahead = [received[i * parts + part + HOP * k] for part in these for k in range(toks - 1)]
        ins = [*local[i], c_flat, growth, gain, decays, *ahead, *inits]
        n_ahead, n_init = len(ahead), len(inits)
        had = y_so_far is not None
        count = len(these) * REQ_CHUNK

        def body(info_ref, *refs):
            local_ref, z_ref, c_ref, growth_ref, gain_ref, decays_ref = refs[:6]
            ahead_refs, init_refs = refs[6 : 6 + n_ahead], refs[6 + n_ahead : 6 + n_ahead + n_init]
            y_ref, token_ref, state_buf, y_buf, sems = refs[-5:]
            token_ref[...] = jnp.zeros_like(token_ref)

            def merge(device):
                for n, part in enumerate(these):
                    for j in range(REQ_CHUNK):
                        r = part * REQ_CHUNK + j
                        value = jnp.zeros((STATE, GROUP_LANES), F32)
                        if device:
                            value = ahead_refs[n * (toks - 1) + device - 1][j].astype(F32)
                        if init_of[device] is not None:
                            started = init_refs[init_of[device]][r].astype(F32) * decay_of(decays_ref, BEFORE, r, group)
                            if unit < GROUP_LANES:
                                lane = lax.broadcasted_iota(jnp.int32, (1, GROUP_LANES), 1) + group * GROUP_LANES
                                started = jnp.where(lane >= device * unit, started, 0.0)
                            value = value + started
                        state_buf[n * REQ_CHUNK + j] = value.astype(BF16)

            on_device(info_ref[0], toks, merge)
            def store(n):
                target = y_ref.at[these[0] * REQ_CHUNK + n, :, pl.ds(group * GROUP_LANES, GROUP_LANES)]
                return pltpu.make_async_copy(y_buf.at[n], target, sems.at[n])

            @pl.loop(0, count)
            def _(n):
                r = these[0] * REQ_CHUNK + n
                valid = info_ref[3 + r] > 0

                @pl.when(jnp.logical_not(valid))
                def _():
                    y_buf[n] = jnp.zeros((span, GROUP_LANES), BF16)

                @pl.when(valid)
                def _():
                    low = low_half(span)
                    c_here = c_ref[r, :, group * STATE : (group + 1) * STATE]
                    carried = jnp.dot(c_here, state_buf[n], preferred_element_type=F32)
                    grown = growth_ref[r, group]
                    gated = []
                    squares = jnp.zeros((span, PAIR_LANES), F32)
                    for q in range(PAIRS):
                        here = pair_lanes(q)
                        summed = local_ref[r, :, here] + carried[:, here] * spread_pair(grown, q, low)
                        gate = z_ref[r, :, here].astype(F32)
                        value = summed.astype(BF16).astype(F32) * (gate / (1.0 + jnp.exp(-gate)))
                        gated.append(value)
                        squares = squares + value * value
                    inverse = lax.rsqrt(jnp.sum(squares, axis=1, keepdims=True) * (1.0 / GROUP_LANES) + EPS)
                    for q in range(PAIRS):
                        first = group * GROUP_LANES + q * PAIR_LANES
                        gain_here = gain_ref[:, first : first + PAIR_LANES]
                        y_buf[n, :, pair_lanes(q)] = (gated[q] * inverse * gain_here).astype(BF16)

                store(n).start()

            @pl.loop(0, count)
            def _(n):
                store(n).wait()

        n_after = len(after)

        def kernel(*refs):
            body(*refs[: 1 + len(ins)], *refs[1 + len(ins) + n_after + had :])

        pinned = [pin(a) for a in (*ins, *after)]
        return pl.pallas_call(
            kernel,
            out_shape=(jax.ShapeDtypeStruct((requests, span, width), BF16), VMEM((8, PAIR_LANES), F32)),
            in_specs=[smem_spec] + [vmem_spec] * len(pinned) + [any_spec] * had,
            out_specs=(any_spec, vmem_spec),
            input_output_aliases={1 + len(pinned): 0} if had else {},
            scratch_shapes=[
                VMEM((count, STATE, GROUP_LANES), BF16),
                VMEM((count, span, GROUP_LANES), BF16),
                pltpu.SemaphoreType.DMA((count,)),
            ],
            compiler_params=pltpu.CompilerParams(vmem_limit_bytes=12 << 20),
            cost_estimate=takes(4.0),
            name="finish",
        )(info, *pinned, *([y_so_far] if had else []))

    def final_states(after):
        initial, decays = started
        ahead = {}
        for k in range(1, toks):
            i = where[k * unit // GROUP_LANES]
            for part in range(parts):
                ahead[k, part] = received[i * parts + part + HOP * (k - 1)]
        keys = list(ahead)
        ins = [decays, initial, arrived[-1], *ahead.values(), *(states[c] for c in range(chunks))]
        n_after = len(after)

        def kernel(ids_ref, *refs):
            decays_ref, initial_ref, later_ref = refs[:3]
            ahead_refs = dict(zip(keys, refs[3 : 3 + len(keys)]))
            state_refs = refs[3 + len(keys) : 3 + len(keys) + chunks]
            final_ref, buf, sems = refs[-4:][:1] + refs[-2:]
            refs[-3][...] = jnp.zeros_like(refs[-3])

            def branch(device):
                first = device * unit
                group, low = first // GROUP_LANES, first % GROUP_LANES
                lanes = slice(low, low + unit)
                for r in range(requests):
                    part, j = r // REQ_CHUNK, r % REQ_CHUNK
                    value = state_refs[where[group] * parts + part][j, :, lanes].astype(F32)
                    value = value + decay_of(decays_ref, BEFORE_THROUGH, r, group, lanes) * initial_ref[r].astype(F32)
                    if device:
                        through = decay_of(decays_ref, THROUGH, r, group, lanes)
                        value = value + through * ahead_refs[device, part][j, :, lanes].astype(F32)
                    value = value * decay_of(decays_ref, AFTER, r, group, lanes)
                    if device < toks - 1:
                        value = value + later_ref[r].astype(F32)
                    buf[r] = value.T

            on_device(ids_ref[0], toks, branch)
            copies = [pltpu.make_async_copy(buf.at[r], final_ref.at[r], sems.at[r]) for r in range(requests)]
            for copy in copies:
                copy.start()
            for copy in copies:
                copy.wait()

        pinned = [pin(a) for a in (*ins, *after)]
        final, token = pl.pallas_call(
            kernel,
            out_shape=(jax.ShapeDtypeStruct((requests, unit, STATE), F32), VMEM((8, PAIR_LANES), F32)),
            in_specs=[pl.BlockSpec(memory_space=SMEM)] + [pl.BlockSpec(memory_space=VMEM)] * len(pinned),
            out_specs=(any_spec, vmem_spec),
            scratch_shapes=[VMEM((requests, unit, STATE), F32), pltpu.SemaphoreType.DMA((requests,))],
            compiler_params=pltpu.CompilerParams(vmem_limit_bytes=12 << 20),
            cost_estimate=takes(2.7),
            name="final_states",
        )(info, *pinned)
        return final.reshape(requests, unit // HEAD_DIM, HEAD_DIM, STATE), token

    slots = chunks + HOP * (toks - 2)
    lag = HOP * (toks - 2) + parts
    started = []

    def start_parents(previous):
        initial = pl.pallas_call(
            lambda *refs: parents_body(requests, *refs[: 5 + len(pieces)], *refs[6 + len(pieces) :]),
            out_shape=VMEM((requests, STATE, unit), BF16),
            in_specs=[smem_spec] * 4 + [hbm_spec] + [vmem_spec] * (len(pieces) + 1),
            out_specs=vmem_spec,
            scratch_shapes=[VMEM((requests, unit, STATE), F32), pltpu.SemaphoreType.DMA((requests,))],
            compiler_params=pltpu.CompilerParams(vmem_limit_bytes=12 << 20),
            cost_estimate=takes(0.5),
            name="parents",
        )(info, parent, state_dev, state_slot, cache_rows, *pieces, pin(previous))
        decays = call(
            decay_body,
            ((4, requests, 1, width), F32),
            (*all_dt, bias, rates),
            scalars=(info,),
            after=(initial,),
            name="decays",
            us=0.4,
        )
        started.extend((initial, decays))
        send_down(0)
        return decays

    local = {}
    previous = c_flat
    merges_early = any(chain_lanes(order[h // parts], 0, unit) is not None for h in range(min(HOP, chunks)))
    if merges_early:
        previous = start_parents(previous)
    for h in range(HOP):
        send_up(h)
    if groups > 1:
        previous = find_states(1, (previous,))
    pending = list(range(groups))
    downs = list(range(1, toks))
    y_out, done, final = None, 0, None
    for h in range(HOP, slots):
        previous = send_up(h, (previous,))
        if downs and h >= round(HOP + (3 + 2 * (toks - 1 - len(downs))) * parts / 2):
            previous = send_down(downs.pop(0), (previous,))
        if h == HOP:
            if not started:
                previous = start_parents(previous)
            for i in range(2, groups):
                previous = find_states(i, (previous,))
        elif pending:
            i = pending.pop(0)
            local[i] = local_sums(i, (previous,))
            previous = local[i][0]
        elif done < groups - 1 and done * parts + lag + 1 <= h:
            y_out, previous = finish(done, list(range(parts)), y_out, (previous,))
            done += 1
    for s in downs:
        previous = send_down(s, (previous,))
    while pending:
        i = pending.pop(0)
        local[i] = local_sums(i, (previous,))
        previous = local[i][0]
    while done < groups - 1:
        y_out, previous = finish(done, list(range(parts)), y_out, (previous,))
        done += 1
    for part in range(parts):
        if part == parts - 1:
            final, previous = final_states((previous,))
        y_out, previous = finish(groups - 1, [part], y_out, (previous,))
    return (y_out, final)


def solution(mesh):
    placed = (
        P(("groups", "rep"), "tok", "cache"),
        P(("groups", "rep"), "tok", "cache"),
        P(("groups", "rep"), "tok", "cache", None),
        P(("groups", "rep"), "tok", "cache", None),
        P(("groups", "rep"), "tok", "cache"),
        P("cache"),
        P("cache"),
        P("cache"),
        P("cache"),
        P(("groups", "cache"), None, "tok", None, None),
        P("groups"),
        P("groups"),
        P("groups"),
        P("groups"),
    )
    return jax.shard_map(
        shards,
        mesh=mesh,
        in_specs=placed,
        out_specs=(
            P(("groups", "rep"), "tok", "cache"),
            P(("groups", "rep"), ("cache", "tok"), None, None),
        ),
        check_vma=False,
    )
```

```python
import functools

import jax
import jax.numpy as jnp
from jax import lax
from jax.experimental import pallas as pl
from jax.experimental.pallas import tpu as pltpu
from jax.sharding import PartitionSpec as P

HEADS = 128
HEAD_DIM = 64
GROUPS = 8
STATE = 128
SPAN = 128
EPS = 1e-05

PER_GROUP = HEADS // GROUPS
GROUP_LANES = PER_GROUP * HEAD_DIM
PAIR_LANES = 2 * HEAD_DIM
PAIRS = PER_GROUP // 2
REQ_CHUNK = 2
HOP = 2
THROUGH, BEFORE, BEFORE_THROUGH, AFTER = range(4)

F32 = jnp.float32
BF16 = jnp.bfloat16
VMEM = pltpu.VMEM
SMEM = pltpu.SMEM


def takes(us):
    return pl.CostEstimate(flops=int(us * 4e9), bytes_accessed=int(us * 14e6), transcendentals=0)


def pin(array):
    return pltpu.with_memory_space_constraint(array, VMEM)


def in_hbm(array):
    return pltpu.with_memory_space_constraint(array, pltpu.HBM)


def call(body, outs, ins, *, scalars=(), after=(), name, us=1.0, scratch=(), limit=12):
    n_scalars, n_ins, n_after = len(scalars), len(ins), len(after)

    def kernel(*refs):
        head = refs[: n_scalars + n_ins]
        body(*head, *refs[n_scalars + n_ins + n_after :])

    space = [pl.BlockSpec(memory_space=SMEM)] * n_scalars + [pl.BlockSpec(memory_space=VMEM)] * (n_ins + n_after)
    pinned = [pin(a) for a in (*ins, *after)]
    single = isinstance(outs[0][0], int)
    outs = (outs,) if single else tuple(outs)
    result = pl.pallas_call(
        kernel,
        out_shape=tuple(VMEM(shape, dtype) for shape, dtype in outs),
        in_specs=space,
        out_specs=(pl.BlockSpec(memory_space=VMEM),) * len(outs),
        scratch_shapes=list(scratch),
        compiler_params=pltpu.CompilerParams(vmem_limit_bytes=limit << 20),
        cost_estimate=takes(us),
        name=name,
    )(*scalars, *pinned)
    return result[0] if single else result


def low_half(rows):
    return lax.broadcasted_iota(jnp.int32, (rows, PAIR_LANES), 1) < HEAD_DIM


def spread_pair(values, q, low):
    return jnp.where(low, values[:, 2 * q : 2 * q + 1], values[:, 2 * q + 1 : 2 * q + 2])


def pair_lanes(q):
    return slice(q * PAIR_LANES, (q + 1) * PAIR_LANES)


def on_device(me, count, branch):
    for device in range(count):
        pl.when(me == device)(functools.partial(branch, device))


def softplus(raw):
    return jnp.maximum(raw, 0.0) + jnp.log1p(jnp.exp(-jnp.abs(raw)))


def front_body(
    order, ids, spans_hbm, b_hbm, dt_hbm, bias_hbm, alog_hbm, skip_hbm, gain_hbm, x_hbm, info, cum_ref, cum_t_ref,
    step_t_ref, weight_ref, growth_ref, x_ref, b_ref, dt_ref, bias_ref, alog_ref, skip_ref, gain_ref, *rest
):
    outs, (raw_b, spans, small_sems, x_sem) = rest[:-4], rest[-4:]
    requests, heads_here, span = dt_ref.shape
    pairs = (
        (spans_hbm, spans), (dt_hbm, dt_ref), (bias_hbm, bias_ref), (alog_hbm, alog_ref), (skip_hbm, skip_ref),
        (gain_hbm, gain_ref), (b_hbm, raw_b),
    )
    small = [pltpu.make_async_copy(source, target, small_sems.at[i]) for i, (source, target) in enumerate(pairs)]
    x_copy = pltpu.make_async_copy(x_hbm.at[:, :, pl.ds(order[0] * GROUP_LANES, GROUP_LANES)], x_ref, x_sem)
    for copy in (*small, x_copy):
        copy.start()
    for i in range(3):
        info[i] = ids[i]
    for copy in small:
        copy.wait()
    rows = lax.broadcasted_iota(jnp.int32, (span, span), 0)
    cols = lax.broadcasted_iota(jnp.int32, (span, span), 1)
    lower = (rows >= cols).astype(F32)
    rate = -jnp.exp(alog_ref[...])
    for r in range(requests):
        blocks = spans[ids[1] * requests + r]
        live = (ids[0] < blocks).astype(jnp.int32)
        info[3 + r] = live
        info[3 + requests + r] = blocks
        step = softplus(dt_ref[r].astype(F32).T + bias_ref[...]) * live.astype(F32)
        cum = jnp.dot(lower, rate * step, precision=lax.Precision.HIGHEST, preferred_element_type=F32)
        weight = jnp.exp(cum[span - 1 : span, :] - cum) * step
        growth = jnp.exp(cum)
        cum_t = cum.T
        step_t = step.T
        for g in range(heads_here // PER_GROUP):
            here = slice(g * PER_GROUP, (g + 1) * PER_GROUP)
            cum_ref[r, g] = cum[:, here]
            weight_ref[r, g] = weight[:, here]
            growth_ref[r, g] = growth[:, here]
            cum_t_ref[r, g] = cum_t[here, :]
            step_t_ref[r, g] = step_t[here, :]
    for r in range(requests):
        b_ref[r] = raw_b[r].reshape(b_ref.shape[1:])
    x_copy.wait()
    block_body(order[0], x_ref, b_ref, weight_ref, *outs)


def decay_body(info, *refs):
    dt_refs, (bias_ref, alog_ref, out_ref) = refs[:-3], refs[-3:]
    toks = len(dt_refs)
    requests, heads_here, _ = dt_refs[0].shape
    width = out_ref.shape[-1]
    me = info[0]
    rate = -jnp.exp(alog_ref[...])

    blank = jnp.zeros((requests, heads_here), F32)
    sums = (blank, blank, blank)
    for n, dt_ref in enumerate(dt_refs):
        t = lax.rem(me - n + toks, toks)
        totals = []
        for r in range(requests):
            step = softplus(dt_ref[r].astype(F32).T + bias_ref[...])
            live = (t < info[3 + requests + r]).astype(F32)
            totals.append(jnp.sum(step, axis=0, keepdims=True) * (rate * live))
        total = jnp.concatenate(totals, axis=0)
        sums = [held + total * chosen.astype(F32) for held, chosen in zip(sums, (me == t, me > t, me < t))]
    through, before, after = sums
    factors = jnp.exp(jnp.concatenate([through, before, before + through, after], axis=0))
    owner = lax.broadcasted_iota(jnp.int32, (heads_here, width), 1) // HEAD_DIM
    head = lax.broadcasted_iota(jnp.int32, (heads_here, width), 0)
    lanes = jnp.dot(
        factors, (owner == head).astype(F32), precision=lax.Precision.HIGHEST, preferred_element_type=F32
    )
    for kind in range(4):
        for r in range(requests):
            row = kind * requests + r
            out_ref[kind, r] = lanes[row : row + 1]


def block_body(group, x_ref, b_ref, weight_ref, *outs):
    low = low_half(x_ref.shape[1])
    for part, out_ref in enumerate(outs):
        for i in range(REQ_CHUNK):
            r = part * REQ_CHUNK + i
            weight = weight_ref[r, group]
            scaled = []
            for q in range(PAIRS):
                here = pair_lanes(q)
                scaled.append((x_ref[r, :, here].astype(F32) * spread_pair(weight, q, low)).astype(BF16))
            b_here = b_ref[r, :, group * STATE : (group + 1) * STATE]
            states = lax.dot_general(
                b_here, jnp.concatenate(scaled, axis=1), (((0,), (0,)), ((), ())), preferred_element_type=F32
            )
            out_ref[i] = states.astype(BF16)


def local_body(group, info, x_ref, b_ref, c_ref, cum_ref, cum_t_ref, step_t_ref, skip_ref, z_hbm, out_ref, z_ref, sem):
    requests, span = x_ref.shape[:2]
    z_copy = pltpu.make_async_copy(z_hbm.at[:, :, pl.ds(group * GROUP_LANES, GROUP_LANES)], z_ref, sem)
    z_copy.start()

    @pl.loop(0, requests)
    def _(r):
        @pl.when(info[3 + r] > 0)
        def _():
            rows = lax.broadcasted_iota(jnp.int32, (span, span), 0)
            cols = lax.broadcasted_iota(jnp.int32, (span, span), 1)
            causal = rows >= cols
            low = low_half(span)
            state = slice(group * STATE, (group + 1) * STATE)
            scores = lax.dot_general(
                c_ref[r, :, state], b_ref[r, :, state], (((1,), (1,)), ((), ())), preferred_element_type=F32
            )
            cum = cum_ref[r, group]
            cum_t = cum_t_ref[r, group]
            step_t = step_t_ref[r, group]

            def mix(h):
                apart = cum[:, h : h + 1] - cum_t[h : h + 1, :]
                decay = jnp.exp(jnp.where(causal, apart, -jnp.inf))
                return (scores * decay * step_t[h : h + 1, :]).astype(BF16)

            for q in range(PAIRS):
                here = pair_lanes(q)
                x_pair = x_ref[r, :, here]
                nothing = jnp.zeros_like(x_pair)
                both = jnp.concatenate([jnp.where(low, x_pair, nothing), jnp.where(low, nothing, x_pair)], axis=0)
                blend = jnp.concatenate([mix(2 * q), mix(2 * q + 1)], axis=1)
                diagonal = jnp.dot(blend, both, preferred_element_type=F32)
                first = group * PER_GROUP + 2 * q
                skip = jnp.where(low[:1], skip_ref[:, first : first + 1], skip_ref[:, first + 1 : first + 2])
                out_ref[r, :, pair_lanes(q)] = diagonal + skip * x_pair.astype(F32)

    z_copy.wait()


def parents_body(requests, info, parent, state_dev, state_slot, cache_hbm, *refs):
    pieces, (out_ref, rows, sems) = refs[:-3], refs[-3:]
    holders = len(pieces) + 1
    places = []
    for r in range(requests):
        kept = parent[info[1] * requests + r]
        places.append((lax.rem(info[2] - state_dev[kept] + holders, holders), state_slot[kept]))

    def own(r, do):
        shift, slot = places[r]

        @pl.when(shift == 0)
        def _():
            do(pltpu.make_async_copy(cache_hbm.at[slot, info[2]], rows.at[r], sems.at[r]))

    for r in range(requests):
        own(r, lambda copy: copy.start())
    for r in range(requests):
        shift, slot = places[r]
        for n, piece in enumerate(pieces):

            @pl.when(shift == n + 1)
            def _(r=r, slot=slot, piece=piece):
                out_ref[r] = piece[slot].T

        own(r, lambda copy: copy.wait())

        @pl.when(shift == 0)
        def _(r=r):
            out_ref[r] = rows[r].astype(BF16).T


def chain_lanes(group, device, unit):
    first = device * unit
    if first // GROUP_LANES != group:
        return None
    low = first % GROUP_LANES
    return slice(low, low + unit)


def shards(
    x_in, z_in, b_in, c_in, dt_in, dt_bias, a_log, skip_gain, norm_w, cache_states, parent, state_dev, state_slot, spans
):
    me = lax.axis_index("tok")
    toks = lax.axis_size("tok")
    holders = lax.axis_size("cache")
    requests, span, width = x_in.shape
    heads_here = dt_in.shape[2]
    groups = width // GROUP_LANES
    parts = requests // REQ_CHUNK
    chunks = groups * parts
    unit = width // toks
    order = [(i + 2) % groups for i in range(groups)]
    where = {group: i for i, group in enumerate(order)}
    assert span == SPAN and GROUP_LANES % unit == 0

    ids = jnp.stack([me, lax.axis_index("rep"), lax.axis_index("cache")]).astype(jnp.int32)


    dt_t = dt_in.transpose(0, 2, 1)
    flat = VMEM((requests, span, groups * STATE), BF16)
    columns = VMEM((requests, groups, span, PER_GROUP), F32)
    as_rows = VMEM((requests, groups, PER_GROUP, span), F32)
    chunk_type = ((REQ_CHUNK, STATE, GROUP_LANES), BF16)
    smem_spec, vmem_spec, any_spec, hbm_spec = (
        pl.BlockSpec(memory_space=space) for space in (SMEM, VMEM, pl.ANY, pltpu.HBM)
    )
    info, cum, cum_t, step_t, weight, growth, x_first, b_flat, dt_here, bias, rates, skip, gain, *found = pl.pallas_call(
        functools.partial(front_body, order),
        out_shape=(
            jax.ShapeDtypeStruct((3 + 2 * requests,), jnp.int32),
            columns, as_rows, as_rows, columns, columns, VMEM((requests, span, GROUP_LANES), BF16), flat, VMEM(dt_t.shape, BF16),
            *(VMEM((1, heads_here), F32),) * 3, VMEM((1, width), F32), *(VMEM(*chunk_type),) * parts,
        ),
        in_specs=[smem_spec] + [hbm_spec] * 8,
        out_specs=(smem_spec,) + (vmem_spec,) * (12 + parts),
        scratch_shapes=[
            VMEM(b_in.shape, BF16), SMEM(spans.shape, jnp.int32),
            pltpu.SemaphoreType.DMA((7,)), pltpu.SemaphoreType.DMA,
        ],
        compiler_params=pltpu.CompilerParams(vmem_limit_bytes=12 << 20),
        cost_estimate=takes(5.0),
        name="front",
    )(
        ids,
        *map(in_hbm, (spans, b_in, dt_t, dt_bias[None], a_log[None], skip_gain[None], norm_w[None], x_in)),
    )
    states = {part: found[part] for part in range(parts)}
    previous = found[-1]

    slots_here = cache_states.shape[0]
    cache_rows = in_hbm(cache_states.reshape(slots_here, holders, unit, STATE))

    def load_body(info_ref, cache_hbm, x_hbm, c_hbm, _, *refs):
        piece_refs, c_ref, x_refs = refs[: holders - 1], refs[holders - 1], refs[holders : holders + groups - 1]
        rows_ref, raw_c, sems = refs[-3:]
        copies = []
        for n in range(holders - 1):
            towards = lax.rem(info_ref[2] + n + 1, holders)
            copies.append(pltpu.make_async_copy(cache_hbm.at[:, towards], rows_ref.at[n], sems.at[n]))
        copies.append(pltpu.make_async_copy(c_hbm, raw_c, sems.at[holders - 1]))
        for n, group in enumerate(order[1:]):
            lanes = pl.ds(group * GROUP_LANES, GROUP_LANES)
            copies.append(pltpu.make_async_copy(x_hbm.at[:, :, lanes], x_refs[n], sems.at[holders + n]))
        for copy in copies:
            copy.start()
        for n in range(holders - 1):
            copies[n].wait()
            piece_refs[n][...] = rows_ref[n].astype(BF16)
        copies[holders - 1].wait()
        for r in range(requests):
            c_ref[r] = raw_c[r].reshape(c_ref.shape[1:])
        for copy in copies[holders:]:
            copy.wait()

    piece_type = (slots_here, unit, STATE)
    loaded = pl.pallas_call(
        load_body,
        out_shape=(VMEM(piece_type, BF16),) * (holders - 1) + (flat,) + (VMEM(x_first.shape, BF16),) * (groups - 1),
        in_specs=[smem_spec] + [hbm_spec] * 3 + [vmem_spec],
        out_specs=(vmem_spec,) * (holders + groups - 1),
        scratch_shapes=[
            VMEM((holders - 1, *piece_type), F32), VMEM(c_in.shape, BF16), pltpu.SemaphoreType.DMA((holders + groups,)),
        ],
        compiler_params=pltpu.CompilerParams(vmem_limit_bytes=12 << 20),
        cost_estimate=takes(3.0),
        name="loads",
    )(info, cache_rows, in_hbm(x_in), in_hbm(c_in), pin(previous))
    all_dt = [dt_here] + [
        lax.ppermute(dt_here, "tok", [(k, (k + shift) % toks) for k in range(toks)]) for shift in range(1, toks)
    ]
    pieces = [
        pin(lax.ppermute(loaded[n], "cache", [(i, (i + n + 1) % holders) for i in range(holders)]))
        for n in range(holders - 1)
    ]
    c_flat, x_groups = loaded[holders - 1], [x_first, *loaded[holders:]]
    def find_states(i, after):
        found = call(
            functools.partial(block_body, order[i]),
            (chunk_type,) * parts,
            (x_groups[i], b_flat, weight),
            after=after,
            name="block_states",
            us=0.4,
        )
        for part in range(parts):
            states[i * parts + part] = found[part]
        return found[-1]

    def decay_of(decays_ref, kind, r, group, lanes=slice(0, GROUP_LANES)):
        return decays_ref[kind, r, :, group * GROUP_LANES + lanes.start : group * GROUP_LANES + lanes.stop]

    received, arrived = {}, []

    def pass_on(h, after):
        devices = [k for k in range(toks - 1) if 0 <= h - HOP * k < chunks]
        if devices == [0] and chain_lanes(order[h // parts], 0, unit) is None:
            return states[h]
        incoming = [received[h - HOP]] if any(devices) else []
        merging = any(chain_lanes(order[(h - HOP * k) // parts], k, unit) is not None for k in devices)
        ins = [states[h - HOP * k] for k in devices] + incoming + [growth] + (started[::-1] if merging else [])

        def body(ids_ref, *refs):
            out_ref = refs[-1]
            state_refs, refs = refs[: len(devices)], refs[len(devices) : -1]
            incoming_ref, refs = (refs[0], refs[1:]) if incoming else (None, refs)
            growth_ref = refs[0]

            def branch(n, device):
                c = h - HOP * device
                group, part = order[c // parts], c % parts
                lanes = chain_lanes(group, device, unit)
                low = low_half(1)
                for i in range(REQ_CHUNK):
                    r = part * REQ_CHUNK + i
                    value = state_refs[n][i].astype(F32)
                    if device:
                        through = growth_ref[r, group, span - 1 : span, :]
                        through = jnp.concatenate([spread_pair(through, q, low) for q in range(PAIRS)], axis=1)
                        value = value + through * incoming_ref[i].astype(F32)
                    out_ref[i] = value.astype(BF16)
                    if lanes is not None:
                        decays_ref, initial_ref = refs[1:]
                        mine = decay_of(decays_ref, BEFORE_THROUGH, r, group, lanes) * initial_ref[r].astype(F32)
                        out_ref[i, :, lanes] = (value[:, lanes] + mine).astype(BF16)

            for n, device in enumerate(devices):
                pl.when(ids_ref[0] == device)(functools.partial(branch, n, device))

        return call(body, chunk_type, ins, scalars=(info,), after=after, name="pass_on", us=0.8)

    def send_up(h, after=()):
        sent = pass_on(h, after)
        pairs = [(k, k + 1) for k in range(toks - 1) if 0 <= h - HOP * k < chunks]
        received[h] = lax.ppermute(sent, "tok", pairs)
        return sent

    backward = [(k, k - 1) for k in range(1, toks)]

    def send_down(s, after=()):
        initial, decays = started
        sent = initial
        if s:
            used = sorted(
                {where[(s - toks + k) * unit // GROUP_LANES] for k in range(1, toks) if s - toks + k >= 0}
            )
            wanted = [i * parts + part for i in used for part in range(parts)]

            def body(ids_ref, decays_ref, incoming_ref, *refs):
                state_refs, out_ref = refs[:-1], refs[-1]

                def branch(device):
                    target = s - toks + device
                    if target < 0:
                        out_ref[...] = incoming_ref[...]
                        return
                    first = target * unit
                    group, low = first // GROUP_LANES, first % GROUP_LANES
                    lanes = slice(low, low + unit)
                    for r in range(requests):
                        chunk = wanted.index(where[group] * parts + r // REQ_CHUNK)
                        state = state_refs[chunk][r % REQ_CHUNK, :, lanes].astype(F32)
                        later = decay_of(decays_ref, AFTER, r, group, lanes) * state
                        if device < toks - 1:
                            later = later + incoming_ref[r].astype(F32)
                        out_ref[r] = later.astype(BF16)

                on_device(ids_ref[0], toks, branch)

            sent = call(
                body,
                ((requests, STATE, unit), BF16),
                [decays, arrived[-1]] + [states[c] for c in wanted],
                scalars=(info,),
                after=after,
                name="pass_down",
                us=0.8,
            )
        arrived.append(lax.ppermute(sent, "tok", backward))
        return sent

    def local_sums(i, after):
        ins = (x_groups[i], b_flat, c_flat, cum, cum_t, step_t, skip)
        n_ins, n_after = len(ins), len(after)
        return pl.pallas_call(
            lambda *refs: local_body(order[i], *refs[: 1 + n_ins], refs[1 + n_ins], *refs[2 + n_ins + n_after :]),
            out_shape=(VMEM((requests, span, GROUP_LANES), F32), VMEM((requests, span, GROUP_LANES), BF16)),
            in_specs=[smem_spec] + [vmem_spec] * n_ins + [hbm_spec] + [vmem_spec] * n_after,
            out_specs=(vmem_spec, vmem_spec),
            scratch_shapes=[pltpu.SemaphoreType.DMA],
            compiler_params=pltpu.CompilerParams(vmem_limit_bytes=12 << 20),
            cost_estimate=takes(1.0),
            name="local_sums",
        )(info, *(pin(a) for a in ins), in_hbm(z_in), *(pin(a) for a in after))

    def init_for(group):
        initial = started[0]
        if unit == GROUP_LANES:
            inits = [initial] + arrived[:group]
            return inits, [group - k if k <= group else None for k in range(toks)]
        stacked = jnp.stack([initial] + arrived[: toks - 1])[lax.rem(jnp.arange(toks) - me + toks, toks)]
        full = stacked.transpose(1, 2, 0, 3).reshape(requests, STATE, width)
        return [full[:, :, group * GROUP_LANES : (group + 1) * GROUP_LANES]], [0] * toks

    def finish(i, these, y_so_far, after):
        group = order[i]
        inits, init_of = init_for(group)
        decays = started[1]
        ahead = [received[i * parts + part + HOP * k] for part in these for k in range(toks - 1)]
        ins = [*local[i], c_flat, growth, gain, decays, *ahead, *inits]
        n_ahead, n_init = len(ahead), len(inits)
        had = y_so_far is not None
        count = len(these) * REQ_CHUNK

        def body(info_ref, *refs):
            local_ref, z_ref, c_ref, growth_ref, gain_ref, decays_ref = refs[:6]
            ahead_refs, init_refs = refs[6 : 6 + n_ahead], refs[6 + n_ahead : 6 + n_ahead + n_init]
            y_ref, token_ref, state_buf, y_buf, sems = refs[-5:]
            token_ref[...] = jnp.zeros_like(token_ref)

            def merge(device):
                for n, part in enumerate(these):
                    for j in range(REQ_CHUNK):
                        r = part * REQ_CHUNK + j
                        value = jnp.zeros((STATE, GROUP_LANES), F32)
                        if device:
                            value = ahead_refs[n * (toks - 1) + device - 1][j].astype(F32)
                        if init_of[device] is not None:
                            started = init_refs[init_of[device]][r].astype(F32) * decay_of(decays_ref, BEFORE, r, group)
                            if unit < GROUP_LANES:
                                lane = lax.broadcasted_iota(jnp.int32, (1, GROUP_LANES), 1) + group * GROUP_LANES
                                started = jnp.where(lane >= device * unit, started, 0.0)
                            value = value + started
                        state_buf[n * REQ_CHUNK + j] = value.astype(BF16)

            on_device(info_ref[0], toks, merge)
            def store(n):
                target = y_ref.at[these[0] * REQ_CHUNK + n, :, pl.ds(group * GROUP_LANES, GROUP_LANES)]
                return pltpu.make_async_copy(y_buf.at[n], target, sems.at[n])

            @pl.loop(0, count)
            def _(n):
                r = these[0] * REQ_CHUNK + n
                valid = info_ref[3 + r] > 0

                @pl.when(jnp.logical_not(valid))
                def _():
                    y_buf[n] = jnp.zeros((span, GROUP_LANES), BF16)

                @pl.when(valid)
                def _():
                    low = low_half(span)
                    c_here = c_ref[r, :, group * STATE : (group + 1) * STATE]
                    carried = jnp.dot(c_here, state_buf[n], preferred_element_type=F32)
                    grown = growth_ref[r, group]
                    gated = []
                    squares = jnp.zeros((span, PAIR_LANES), F32)
                    for q in range(PAIRS):
                        here = pair_lanes(q)
                        summed = local_ref[r, :, here] + carried[:, here] * spread_pair(grown, q, low)
                        gate = z_ref[r, :, here].astype(F32)
                        value = summed.astype(BF16).astype(F32) * (gate / (1.0 + jnp.exp(-gate)))
                        gated.append(value)
                        squares = squares + value * value
                    inverse = lax.rsqrt(jnp.sum(squares, axis=1, keepdims=True) * (1.0 / GROUP_LANES) + EPS)
                    for q in range(PAIRS):
                        first = group * GROUP_LANES + q * PAIR_LANES
                        gain_here = gain_ref[:, first : first + PAIR_LANES]
                        y_buf[n, :, pair_lanes(q)] = (gated[q] * inverse * gain_here).astype(BF16)

                store(n).start()

            @pl.loop(0, count)
            def _(n):
                store(n).wait()

        n_after = len(after)

        def kernel(*refs):
            body(*refs[: 1 + len(ins)], *refs[1 + len(ins) + n_after + had :])

        pinned = [pin(a) for a in (*ins, *after)]
        return pl.pallas_call(
            kernel,
            out_shape=(jax.ShapeDtypeStruct((requests, span, width), BF16), VMEM((8, PAIR_LANES), F32)),
            in_specs=[smem_spec] + [vmem_spec] * len(pinned) + [any_spec] * had,
            out_specs=(any_spec, vmem_spec),
            input_output_aliases={1 + len(pinned): 0} if had else {},
            scratch_shapes=[
                VMEM((count, STATE, GROUP_LANES), BF16),
                VMEM((count, span, GROUP_LANES), BF16),
                pltpu.SemaphoreType.DMA((count,)),
            ],
            compiler_params=pltpu.CompilerParams(vmem_limit_bytes=12 << 20),
            cost_estimate=takes(1.5),
            name="finish",
        )(info, *pinned, *([y_so_far] if had else []))

    def final_states(after):
        initial, decays = started
        ahead = {}
        for k in range(1, toks):
            i = where[k * unit // GROUP_LANES]
            for part in range(parts):
                ahead[k, part] = received[i * parts + part + HOP * (k - 1)]
        keys = list(ahead)
        ins = [decays, initial, arrived[-1], *ahead.values(), *(states[c] for c in range(chunks))]
        n_after = len(after)

        def kernel(ids_ref, *refs):
            decays_ref, initial_ref, later_ref = refs[:3]
            ahead_refs = dict(zip(keys, refs[3 : 3 + len(keys)]))
            state_refs = refs[3 + len(keys) : 3 + len(keys) + chunks]
            final_ref, buf, sems = refs[-4:][:1] + refs[-2:]
            refs[-3][...] = jnp.zeros_like(refs[-3])

            def branch(device):
                first = device * unit
                group, low = first // GROUP_LANES, first % GROUP_LANES
                lanes = slice(low, low + unit)
                for r in range(requests):
                    part, j = r // REQ_CHUNK, r % REQ_CHUNK
                    value = state_refs[where[group] * parts + part][j, :, lanes].astype(F32)
                    value = value + decay_of(decays_ref, BEFORE_THROUGH, r, group, lanes) * initial_ref[r].astype(F32)
                    if device:
                        through = decay_of(decays_ref, THROUGH, r, group, lanes)
                        value = value + through * ahead_refs[device, part][j, :, lanes].astype(F32)
                    value = value * decay_of(decays_ref, AFTER, r, group, lanes)
                    if device < toks - 1:
                        value = value + later_ref[r].astype(F32)
                    buf[r] = value.T

            on_device(ids_ref[0], toks, branch)
            copies = [pltpu.make_async_copy(buf.at[r], final_ref.at[r], sems.at[r]) for r in range(requests)]
            for copy in copies:
                copy.start()
            for copy in copies:
                copy.wait()

        pinned = [pin(a) for a in (*ins, *after)]
        final, token = pl.pallas_call(
            kernel,
            out_shape=(jax.ShapeDtypeStruct((requests, unit, STATE), F32), VMEM((8, PAIR_LANES), F32)),
            in_specs=[pl.BlockSpec(memory_space=SMEM)] + [pl.BlockSpec(memory_space=VMEM)] * len(pinned),
            out_specs=(any_spec, vmem_spec),
            scratch_shapes=[VMEM((requests, unit, STATE), F32), pltpu.SemaphoreType.DMA((requests,))],
            compiler_params=pltpu.CompilerParams(vmem_limit_bytes=12 << 20),
            cost_estimate=takes(2.7),
            name="final_states",
        )(info, *pinned)
        return final.reshape(requests, unit // HEAD_DIM, HEAD_DIM, STATE), token

    slots = chunks + HOP * (toks - 2)
    lag = HOP * (toks - 2) + parts
    started = []

    def start_parents(previous):
        initial = pl.pallas_call(
            lambda *refs: parents_body(requests, *refs[: 5 + len(pieces)], *refs[6 + len(pieces) :]),
            out_shape=VMEM((requests, STATE, unit), BF16),
            in_specs=[smem_spec] * 4 + [hbm_spec] + [vmem_spec] * (len(pieces) + 1),
            out_specs=vmem_spec,
            scratch_shapes=[VMEM((requests, unit, STATE), F32), pltpu.SemaphoreType.DMA((requests,))],
            compiler_params=pltpu.CompilerParams(vmem_limit_bytes=12 << 20),
            cost_estimate=takes(0.5),
            name="parents",
        )(info, parent, state_dev, state_slot, cache_rows, *pieces, pin(previous))
        decays = call(
            decay_body,
            ((4, requests, 1, width), F32),
            (*all_dt, bias, rates),
            scalars=(info,),
            after=(initial,),
            name="decays",
            us=0.4,
        )
        started.extend((initial, decays))
        send_down(0)
        return decays

    local = {}
    previous = c_flat
    merges_early = any(chain_lanes(order[h // parts], 0, unit) is not None for h in range(min(HOP, chunks)))
    if merges_early:
        previous = start_parents(previous)
    for h in range(HOP):
        send_up(h)
    if groups > 1:
        previous = find_states(1, (previous,))
    pending = list(range(groups))
    downs = list(range(1, toks))
    y_out, done, final = None, 0, None
    for h in range(HOP, slots):
        previous = send_up(h, (previous,))
        if downs and h >= round(HOP + (3 + 2 * (toks - 1 - len(downs))) * parts / 2):
            previous = send_down(downs.pop(0), (previous,))
        if h == HOP:
            if not started:
                previous = start_parents(previous)
            for i in range(2, groups):
                previous = find_states(i, (previous,))
        elif pending:
            i = pending.pop(0)
            local[i] = local_sums(i, (previous,))
            previous = local[i][0]
        elif done < groups - 1 and done * parts + lag + 1 <= h:
            y_out, previous = finish(done, list(range(parts)), y_out, (previous,))
            done += 1
    for s in downs:
        previous = send_down(s, (previous,))
    while pending:
        i = pending.pop(0)
        local[i] = local_sums(i, (previous,))
        previous = local[i][0]
    while done < groups - 1:
        y_out, previous = finish(done, list(range(parts)), y_out, (previous,))
        done += 1
    for part in range(parts):
        if part == parts - 1:
            final, previous = final_states((previous,))
        y_out, previous = finish(groups - 1, [part], y_out, (previous,))
    return (y_out, final)


def solution(mesh):
    placed = (
        P(("groups", "rep"), "tok", "cache"),
        P(("groups", "rep"), "tok", "cache"),
        P(("groups", "rep"), "tok", "cache", None),
        P(("groups", "rep"), "tok", "cache", None),
        P(("groups", "rep"), "tok", "cache"),
        P("cache"),
        P("cache"),
        P("cache"),
        P("cache"),
        P(("groups", "cache"), None, "tok", None, None),
        P("groups"),
        P("groups"),
        P("groups"),
        P("groups"),
    )
    return jax.shard_map(
        shards,
        mesh=mesh,
        in_specs=placed,
        out_specs=(
            P(("groups", "rep"), "tok", "cache"),
            P(("groups", "rep"), ("cache", "tok"), None, None),
        ),
        check_vma=False,
    )
```

```python
import functools

import jax
import jax.numpy as jnp
from jax import lax
from jax.experimental import pallas as pl
from jax.experimental.pallas import tpu as pltpu
from jax.sharding import PartitionSpec as P

HEADS = 128
HEAD_DIM = 64
GROUPS = 8
STATE = 128
SPAN = 128
EPS = 1e-05

PER_GROUP = HEADS // GROUPS
GROUP_LANES = PER_GROUP * HEAD_DIM
PAIR_LANES = 2 * HEAD_DIM
PAIRS = PER_GROUP // 2
REQ_CHUNK = 2
HOP = 2
THROUGH, BEFORE, BEFORE_THROUGH, AFTER = range(4)

F32 = jnp.float32
BF16 = jnp.bfloat16
VMEM = pltpu.VMEM
SMEM = pltpu.SMEM


def takes(us):
    return pl.CostEstimate(flops=int(us * 4e9), bytes_accessed=int(us * 14e6), transcendentals=0)


def pin(array):
    return pltpu.with_memory_space_constraint(array, VMEM)


def in_hbm(array):
    return pltpu.with_memory_space_constraint(array, pltpu.HBM)


def call(body, outs, ins, *, scalars=(), after=(), name, us=1.0, scratch=(), limit=12):
    n_scalars, n_ins, n_after = len(scalars), len(ins), len(after)

    def kernel(*refs):
        head = refs[: n_scalars + n_ins]
        body(*head, *refs[n_scalars + n_ins + n_after :])

    space = [pl.BlockSpec(memory_space=SMEM)] * n_scalars + [pl.BlockSpec(memory_space=VMEM)] * (n_ins + n_after)
    pinned = [pin(a) for a in (*ins, *after)]
    single = isinstance(outs[0][0], int)
    outs = (outs,) if single else tuple(outs)
    result = pl.pallas_call(
        kernel,
        out_shape=tuple(VMEM(shape, dtype) for shape, dtype in outs),
        in_specs=space,
        out_specs=(pl.BlockSpec(memory_space=VMEM),) * len(outs),
        scratch_shapes=list(scratch),
        compiler_params=pltpu.CompilerParams(vmem_limit_bytes=limit << 20),
        cost_estimate=takes(us),
        name=name,
    )(*scalars, *pinned)
    return result[0] if single else result


def low_half(rows):
    return lax.broadcasted_iota(jnp.int32, (rows, PAIR_LANES), 1) < HEAD_DIM


def spread_pair(values, q, low):
    return jnp.where(low, values[:, 2 * q : 2 * q + 1], values[:, 2 * q + 1 : 2 * q + 2])


def pair_lanes(q):
    return slice(q * PAIR_LANES, (q + 1) * PAIR_LANES)


def on_device(me, count, branch):
    for device in range(count):
        pl.when(me == device)(functools.partial(branch, device))


def softplus(raw):
    return jnp.maximum(raw, 0.0) + jnp.log1p(jnp.exp(-jnp.abs(raw)))


def front_body(
    order, ids, spans_hbm, b_hbm, dt_hbm, bias_hbm, alog_hbm, skip_hbm, gain_hbm, x_hbm, info, cum_ref, cum_t_ref,
    step_t_ref, weight_ref, growth_ref, x_ref, b_ref, dt_ref, bias_ref, alog_ref, skip_ref, gain_ref, *rest
):
    outs, (raw_b, spans, small_sems, x_sem) = rest[:-4], rest[-4:]
    requests, heads_here, span = dt_ref.shape
    pairs = (
        (spans_hbm, spans), (dt_hbm, dt_ref), (bias_hbm, bias_ref), (alog_hbm, alog_ref), (skip_hbm, skip_ref),
        (gain_hbm, gain_ref), (b_hbm, raw_b),
    )
    small = [pltpu.make_async_copy(source, target, small_sems.at[i]) for i, (source, target) in enumerate(pairs)]
    x_copy = pltpu.make_async_copy(x_hbm.at[:, :, pl.ds(order[0] * GROUP_LANES, GROUP_LANES)], x_ref, x_sem)
    for copy in (*small, x_copy):
        copy.start()
    for i in range(3):
        info[i] = ids[i]
    for copy in small:
        copy.wait()
    rows = lax.broadcasted_iota(jnp.int32, (span, span), 0)
    cols = lax.broadcasted_iota(jnp.int32, (span, span), 1)
    lower = (rows >= cols).astype(F32)
    rate = -jnp.exp(alog_ref[...])
    for r in range(requests):
        blocks = spans[ids[1] * requests + r]
        live = (ids[0] < blocks).astype(jnp.int32)
        info[3 + r] = live
        info[3 + requests + r] = blocks
        step = softplus(dt_ref[r].astype(F32).T + bias_ref[...]) * live.astype(F32)
        cum = jnp.dot(lower, rate * step, precision=lax.Precision.HIGHEST, preferred_element_type=F32)
        weight = jnp.exp(cum[span - 1 : span, :] - cum) * step
        growth = jnp.exp(cum)
        cum_t = cum.T
        step_t = step.T
        for g in range(heads_here // PER_GROUP):
            here = slice(g * PER_GROUP, (g + 1) * PER_GROUP)
            cum_ref[r, g] = cum[:, here]
            weight_ref[r, g] = weight[:, here]
            growth_ref[r, g] = growth[:, here]
            cum_t_ref[r, g] = cum_t[here, :]
            step_t_ref[r, g] = step_t[here, :]
    for r in range(requests):
        b_ref[r] = raw_b[r].reshape(b_ref.shape[1:])
    x_copy.wait()
    block_body(order[0], x_ref, b_ref, weight_ref, *outs)


def decay_body(info, *refs):
    dt_refs, (bias_ref, alog_ref, out_ref) = refs[:-3], refs[-3:]
    toks = len(dt_refs)
    requests, heads_here, _ = dt_refs[0].shape
    width = out_ref.shape[-1]
    me = info[0]
    rate = -jnp.exp(alog_ref[...])

    blank = jnp.zeros((requests, heads_here), F32)
    sums = (blank, blank, blank)
    for n, dt_ref in enumerate(dt_refs):
        t = lax.rem(me - n + toks, toks)
        totals = []
        for r in range(requests):
            step = softplus(dt_ref[r].astype(F32).T + bias_ref[...])
            live = (t < info[3 + requests + r]).astype(F32)
            totals.append(jnp.sum(step, axis=0, keepdims=True) * (rate * live))
        total = jnp.concatenate(totals, axis=0)
        sums = [held + total * chosen.astype(F32) for held, chosen in zip(sums, (me == t, me > t, me < t))]
    through, before, after = sums
    factors = jnp.exp(jnp.concatenate([through, before, before + through, after], axis=0))
    owner = lax.broadcasted_iota(jnp.int32, (heads_here, width), 1) // HEAD_DIM
    head = lax.broadcasted_iota(jnp.int32, (heads_here, width), 0)
    lanes = jnp.dot(
        factors, (owner == head).astype(F32), precision=lax.Precision.HIGHEST, preferred_element_type=F32
    )
    for kind in range(4):
        for r in range(requests):
            row = kind * requests + r
            out_ref[kind, r] = lanes[row : row + 1]


def block_body(group, x_ref, b_ref, weight_ref, *outs):
    low = low_half(x_ref.shape[1])
    for part, out_ref in enumerate(outs):
        for i in range(REQ_CHUNK):
            r = part * REQ_CHUNK + i
            weight = weight_ref[r, group]
            scaled = []
            for q in range(PAIRS):
                here = pair_lanes(q)
                scaled.append((x_ref[r, :, here].astype(F32) * spread_pair(weight, q, low)).astype(BF16))
            b_here = b_ref[r, :, group * STATE : (group + 1) * STATE]
            states = lax.dot_general(
                b_here, jnp.concatenate(scaled, axis=1), (((0,), (0,)), ((), ())), preferred_element_type=F32
            )
            out_ref[i] = states.astype(BF16)


def local_body(group, info, x_ref, b_ref, c_ref, cum_ref, cum_t_ref, step_t_ref, skip_ref, z_hbm, out_ref, z_ref, sem):
    requests, span = x_ref.shape[:2]
    z_copy = pltpu.make_async_copy(z_hbm.at[:, :, pl.ds(group * GROUP_LANES, GROUP_LANES)], z_ref, sem)
    z_copy.start()

    @pl.loop(0, requests)
    def _(r):
        @pl.when(info[3 + r] > 0)
        def _():
            rows = lax.broadcasted_iota(jnp.int32, (span, span), 0)
            cols = lax.broadcasted_iota(jnp.int32, (span, span), 1)
            causal = rows >= cols
            low = low_half(span)
            state = slice(group * STATE, (group + 1) * STATE)
            scores = lax.dot_general(
                c_ref[r, :, state], b_ref[r, :, state], (((1,), (1,)), ((), ())), preferred_element_type=F32
            )
            cum = cum_ref[r, group]
            cum_t = cum_t_ref[r, group]
            step_t = step_t_ref[r, group]

            def mix(h):
                apart = cum[:, h : h + 1] - cum_t[h : h + 1, :]
                decay = jnp.exp(jnp.where(causal, apart, -jnp.inf))
                return (scores * decay * step_t[h : h + 1, :]).astype(BF16)

            for q in range(PAIRS):
                here = pair_lanes(q)
                x_pair = x_ref[r, :, here]
                nothing = jnp.zeros_like(x_pair)
                both = jnp.concatenate([jnp.where(low, x_pair, nothing), jnp.where(low, nothing, x_pair)], axis=0)
                blend = jnp.concatenate([mix(2 * q), mix(2 * q + 1)], axis=1)
                diagonal = jnp.dot(blend, both, preferred_element_type=F32)
                first = group * PER_GROUP + 2 * q
                skip = jnp.where(low[:1], skip_ref[:, first : first + 1], skip_ref[:, first + 1 : first + 2])
                out_ref[r, :, pair_lanes(q)] = diagonal + skip * x_pair.astype(F32)

    z_copy.wait()


def parents_body(requests, info, parent, state_dev, state_slot, cache_hbm, *refs):
    pieces, (out_ref, rows, sems) = refs[:-3], refs[-3:]
    holders = len(pieces) + 1
    places = []
    for r in range(requests):
        kept = parent[info[1] * requests + r]
        places.append((lax.rem(info[2] - state_dev[kept] + holders, holders), state_slot[kept]))

    def own(r, do):
        shift, slot = places[r]

        @pl.when(shift == 0)
        def _():
            do(pltpu.make_async_copy(cache_hbm.at[slot, info[2]], rows.at[r], sems.at[r]))

    for r in range(requests):
        own(r, lambda copy: copy.start())
    for r in range(requests):
        shift, slot = places[r]
        for n, piece in enumerate(pieces):

            @pl.when(shift == n + 1)
            def _(r=r, slot=slot, piece=piece):
                out_ref[r] = piece[slot].T

        own(r, lambda copy: copy.wait())

        @pl.when(shift == 0)
        def _(r=r):
            out_ref[r] = rows[r].astype(BF16).T


def chain_lanes(group, device, unit):
    first = device * unit
    if first // GROUP_LANES != group:
        return None
    low = first % GROUP_LANES
    return slice(low, low + unit)


def shards(
    x_in, z_in, b_in, c_in, dt_in, dt_bias, a_log, skip_gain, norm_w, cache_states, parent, state_dev, state_slot, spans
):
    me = lax.axis_index("tok")
    toks = lax.axis_size("tok")
    holders = lax.axis_size("cache")
    requests, span, width = x_in.shape
    heads_here = dt_in.shape[2]
    groups = width // GROUP_LANES
    parts = requests // REQ_CHUNK
    chunks = groups * parts
    unit = width // toks
    order = [(i + 2) % groups for i in range(groups)]
    where = {group: i for i, group in enumerate(order)}
    assert span == SPAN and GROUP_LANES % unit == 0

    ids = jnp.stack([me, lax.axis_index("rep"), lax.axis_index("cache")]).astype(jnp.int32)


    dt_t = dt_in.transpose(0, 2, 1)
    flat = VMEM((requests, span, groups * STATE), BF16)
    columns = VMEM((requests, groups, span, PER_GROUP), F32)
    as_rows = VMEM((requests, groups, PER_GROUP, span), F32)
    chunk_type = ((REQ_CHUNK, STATE, GROUP_LANES), BF16)
    smem_spec, vmem_spec, any_spec, hbm_spec = (
        pl.BlockSpec(memory_space=space) for space in (SMEM, VMEM, pl.ANY, pltpu.HBM)
    )
    info, cum, cum_t, step_t, weight, growth, x_first, b_flat, dt_here, bias, rates, skip, gain, *found = pl.pallas_call(
        functools.partial(front_body, order),
        out_shape=(
            jax.ShapeDtypeStruct((3 + 2 * requests,), jnp.int32),
            columns, as_rows, as_rows, columns, columns, VMEM((requests, span, GROUP_LANES), BF16), flat, VMEM(dt_t.shape, BF16),
            *(VMEM((1, heads_here), F32),) * 3, VMEM((1, width), F32), *(VMEM(*chunk_type),) * parts,
        ),
        in_specs=[smem_spec] + [hbm_spec] * 8,
        out_specs=(smem_spec,) + (vmem_spec,) * (12 + parts),
        scratch_shapes=[
            VMEM(b_in.shape, BF16), SMEM(spans.shape, jnp.int32),
            pltpu.SemaphoreType.DMA((7,)), pltpu.SemaphoreType.DMA,
        ],
        compiler_params=pltpu.CompilerParams(vmem_limit_bytes=12 << 20),
        cost_estimate=takes(5.0),
        name="front",
    )(
        ids,
        *map(in_hbm, (spans, b_in, dt_t, dt_bias[None], a_log[None], skip_gain[None], norm_w[None], x_in)),
    )
    states = {part: found[part] for part in range(parts)}
    previous = found[-1]

    slots_here = cache_states.shape[0]
    cache_rows = in_hbm(cache_states.reshape(slots_here, holders, unit, STATE))

    def load_body(info_ref, cache_hbm, x_hbm, c_hbm, _, *refs):
        piece_refs, c_ref, x_refs = refs[: holders - 1], refs[holders - 1], refs[holders : holders + groups - 1]
        rows_ref, raw_c, sems = refs[-3:]
        copies = []
        for n in range(holders - 1):
            towards = lax.rem(info_ref[2] + n + 1, holders)
            copies.append(pltpu.make_async_copy(cache_hbm.at[:, towards], rows_ref.at[n], sems.at[n]))
        copies.append(pltpu.make_async_copy(c_hbm, raw_c, sems.at[holders - 1]))
        for n, group in enumerate(order[1:]):
            lanes = pl.ds(group * GROUP_LANES, GROUP_LANES)
            copies.append(pltpu.make_async_copy(x_hbm.at[:, :, lanes], x_refs[n], sems.at[holders + n]))
        for copy in copies:
            copy.start()
        for n in range(holders - 1):
            copies[n].wait()
            piece_refs[n][...] = rows_ref[n].astype(BF16)
        copies[holders - 1].wait()
        for r in range(requests):
            c_ref[r] = raw_c[r].reshape(c_ref.shape[1:])
        for copy in copies[holders:]:
            copy.wait()

    piece_type = (slots_here, unit, STATE)
    loaded = pl.pallas_call(
        load_body,
        out_shape=(VMEM(piece_type, BF16),) * (holders - 1) + (flat,) + (VMEM(x_first.shape, BF16),) * (groups - 1),
        in_specs=[smem_spec] + [hbm_spec] * 3 + [vmem_spec],
        out_specs=(vmem_spec,) * (holders + groups - 1),
        scratch_shapes=[
            VMEM((holders - 1, *piece_type), F32), VMEM(c_in.shape, BF16), pltpu.SemaphoreType.DMA((holders + groups,)),
        ],
        compiler_params=pltpu.CompilerParams(vmem_limit_bytes=12 << 20),
        cost_estimate=takes(3.0),
        name="loads",
    )(info, cache_rows, in_hbm(x_in), in_hbm(c_in), pin(previous))
    all_dt = [dt_here] + [
        lax.ppermute(dt_here, "tok", [(k, (k + shift) % toks) for k in range(toks)]) for shift in range(1, toks)
    ]
    pieces = [
        pin(lax.ppermute(loaded[n], "cache", [(i, (i + n + 1) % holders) for i in range(holders)]))
        for n in range(holders - 1)
    ]
    c_flat, x_groups = loaded[holders - 1], [x_first, *loaded[holders:]]
    def find_states(i, after):
        found = call(
            functools.partial(block_body, order[i]),
            (chunk_type,) * parts,
            (x_groups[i], b_flat, weight),
            after=after,
            name="block_states",
            us=0.4,
        )
        for part in range(parts):
            states[i * parts + part] = found[part]
        return found[-1]

    def decay_of(decays_ref, kind, r, group, lanes=slice(0, GROUP_LANES)):
        return decays_ref[kind, r, :, group * GROUP_LANES + lanes.start : group * GROUP_LANES + lanes.stop]

    received, arrived = {}, []

    def pass_on(h, after):
        devices = [k for k in range(toks - 1) if 0 <= h - HOP * k < chunks]
        if devices == [0] and chain_lanes(order[h // parts], 0, unit) is None:
            return states[h]
        incoming = [received[h - HOP]] if any(devices) else []
        merging = any(chain_lanes(order[(h - HOP * k) // parts], k, unit) is not None for k in devices)
        ins = [states[h - HOP * k] for k in devices] + incoming + [growth] + (started[::-1] if merging else [])

        def body(ids_ref, *refs):
            out_ref = refs[-1]
            state_refs, refs = refs[: len(devices)], refs[len(devices) : -1]
            incoming_ref, refs = (refs[0], refs[1:]) if incoming else (None, refs)
            growth_ref = refs[0]

            def branch(n, device):
                c = h - HOP * device
                group, part = order[c // parts], c % parts
                lanes = chain_lanes(group, device, unit)
                low = low_half(1)
                for i in range(REQ_CHUNK):
                    r = part * REQ_CHUNK + i
                    value = state_refs[n][i].astype(F32)
                    if device:
                        through = growth_ref[r, group, span - 1 : span, :]
                        through = jnp.concatenate([spread_pair(through, q, low) for q in range(PAIRS)], axis=1)
                        value = value + through * incoming_ref[i].astype(F32)
                    out_ref[i] = value.astype(BF16)
                    if lanes is not None:
                        decays_ref, initial_ref = refs[1:]
                        mine = decay_of(decays_ref, BEFORE_THROUGH, r, group, lanes) * initial_ref[r].astype(F32)
                        out_ref[i, :, lanes] = (value[:, lanes] + mine).astype(BF16)

            for n, device in enumerate(devices):
                pl.when(ids_ref[0] == device)(functools.partial(branch, n, device))

        return call(body, chunk_type, ins, scalars=(info,), after=after, name="pass_on", us=0.8)

    def send_up(h, after=()):
        sent = pass_on(h, after)
        pairs = [(k, k + 1) for k in range(toks - 1) if 0 <= h - HOP * k < chunks]
        received[h] = lax.ppermute(sent, "tok", pairs)
        return sent

    backward = [(k, k - 1) for k in range(1, toks)]

    def send_down(s, after=()):
        initial, decays = started
        sent = initial
        if s:
            used = sorted(
                {where[(s - toks + k) * unit // GROUP_LANES] for k in range(1, toks) if s - toks + k >= 0}
            )
            wanted = [i * parts + part for i in used for part in range(parts)]

            def body(ids_ref, decays_ref, incoming_ref, *refs):
                state_refs, out_ref = refs[:-1], refs[-1]

                def branch(device):
                    target = s - toks + device
                    if target < 0:
                        out_ref[...] = incoming_ref[...]
                        return
                    first = target * unit
                    group, low = first // GROUP_LANES, first % GROUP_LANES
                    lanes = slice(low, low + unit)
                    for r in range(requests):
                        chunk = wanted.index(where[group] * parts + r // REQ_CHUNK)
                        state = state_refs[chunk][r % REQ_CHUNK, :, lanes].astype(F32)
                        later = decay_of(decays_ref, AFTER, r, group, lanes) * state
                        if device < toks - 1:
                            later = later + incoming_ref[r].astype(F32)
                        out_ref[r] = later.astype(BF16)

                on_device(ids_ref[0], toks, branch)

            sent = call(
                body,
                ((requests, STATE, unit), BF16),
                [decays, arrived[-1]] + [states[c] for c in wanted],
                scalars=(info,),
                after=after,
                name="pass_down",
                us=0.8,
            )
        arrived.append(lax.ppermute(sent, "tok", backward))
        return sent

    def local_sums(i, after):
        ins = (x_groups[i], b_flat, c_flat, cum, cum_t, step_t, skip)
        n_ins, n_after = len(ins), len(after)
        return pl.pallas_call(
            lambda *refs: local_body(order[i], *refs[: 1 + n_ins], refs[1 + n_ins], *refs[2 + n_ins + n_after :]),
            out_shape=(VMEM((requests, span, GROUP_LANES), F32), VMEM((requests, span, GROUP_LANES), BF16)),
            in_specs=[smem_spec] + [vmem_spec] * n_ins + [hbm_spec] + [vmem_spec] * n_after,
            out_specs=(vmem_spec, vmem_spec),
            scratch_shapes=[pltpu.SemaphoreType.DMA],
            compiler_params=pltpu.CompilerParams(vmem_limit_bytes=12 << 20),
            cost_estimate=takes(1.0),
            name="local_sums",
        )(info, *(pin(a) for a in ins), in_hbm(z_in), *(pin(a) for a in after))

    def init_for(group):
        initial = started[0]
        if unit == GROUP_LANES:
            inits = [initial] + arrived[:group]
            return inits, [group - k if k <= group else None for k in range(toks)]
        stacked = jnp.stack([initial] + arrived[: toks - 1])[lax.rem(jnp.arange(toks) - me + toks, toks)]
        full = stacked.transpose(1, 2, 0, 3).reshape(requests, STATE, width)
        return [full[:, :, group * GROUP_LANES : (group + 1) * GROUP_LANES]], [0] * toks

    def finish(i, these, y_so_far, after):
        group = order[i]
        inits, init_of = init_for(group)
        decays = started[1]
        ahead = [received[i * parts + part + HOP * k] for part in these for k in range(toks - 1)]
        ins = [*local[i], c_flat, growth, gain, decays, *ahead, *inits]
        n_ahead, n_init = len(ahead), len(inits)
        had = y_so_far is not None
        count = len(these) * REQ_CHUNK

        def body(info_ref, *refs):
            local_ref, z_ref, c_ref, growth_ref, gain_ref, decays_ref = refs[:6]
            ahead_refs, init_refs = refs[6 : 6 + n_ahead], refs[6 + n_ahead : 6 + n_ahead + n_init]
            y_ref, token_ref, state_buf, y_buf, sems = refs[-5:]
            token_ref[...] = jnp.zeros_like(token_ref)

            def merge(device):
                for n, part in enumerate(these):
                    for j in range(REQ_CHUNK):
                        r = part * REQ_CHUNK + j
                        value = jnp.zeros((STATE, GROUP_LANES), F32)
                        if device:
                            value = ahead_refs[n * (toks - 1) + device - 1][j].astype(F32)
                        if init_of[device] is not None:
                            started = init_refs[init_of[device]][r].astype(F32) * decay_of(decays_ref, BEFORE, r, group)
                            if unit < GROUP_LANES:
                                lane = lax.broadcasted_iota(jnp.int32, (1, GROUP_LANES), 1) + group * GROUP_LANES
                                started = jnp.where(lane >= device * unit, started, 0.0)
                            value = value + started
                        state_buf[n * REQ_CHUNK + j] = value.astype(BF16)

            on_device(info_ref[0], toks, merge)
            def store(n):
                target = y_ref.at[these[0] * REQ_CHUNK + n, :, pl.ds(group * GROUP_LANES, GROUP_LANES)]
                return pltpu.make_async_copy(y_buf.at[n], target, sems.at[n])

            @pl.loop(0, count)
            def _(n):
                r = these[0] * REQ_CHUNK + n
                valid = info_ref[3 + r] > 0

                @pl.when(jnp.logical_not(valid))
                def _():
                    y_buf[n] = jnp.zeros((span, GROUP_LANES), BF16)

                @pl.when(valid)
                def _():
                    low = low_half(span)
                    c_here = c_ref[r, :, group * STATE : (group + 1) * STATE]
                    carried = jnp.dot(c_here, state_buf[n], preferred_element_type=F32)
                    grown = growth_ref[r, group]
                    gated = []
                    squares = jnp.zeros((span, PAIR_LANES), F32)
                    for q in range(PAIRS):
                        here = pair_lanes(q)
                        summed = local_ref[r, :, here] + carried[:, here] * spread_pair(grown, q, low)
                        half = 0.5 * z_ref[r, :, here].astype(F32)
                        value = summed.astype(BF16).astype(F32) * (half + half * jnp.tanh(half))
                        gated.append(value)
                        squares = squares + value * value
                    inverse = lax.rsqrt(jnp.sum(squares, axis=1, keepdims=True) * (1.0 / GROUP_LANES) + EPS)
                    for q in range(PAIRS):
                        first = group * GROUP_LANES + q * PAIR_LANES
                        gain_here = gain_ref[:, first : first + PAIR_LANES]
                        y_buf[n, :, pair_lanes(q)] = (gated[q] * inverse * gain_here).astype(BF16)

                store(n).start()

            @pl.loop(0, count)
            def _(n):
                store(n).wait()

        n_after = len(after)

        def kernel(*refs):
            body(*refs[: 1 + len(ins)], *refs[1 + len(ins) + n_after + had :])

        pinned = [pin(a) for a in (*ins, *after)]
        return pl.pallas_call(
            kernel,
            out_shape=(jax.ShapeDtypeStruct((requests, span, width), BF16), VMEM((8, PAIR_LANES), F32)),
            in_specs=[smem_spec] + [vmem_spec] * len(pinned) + [any_spec] * had,
            out_specs=(any_spec, vmem_spec),
            input_output_aliases={1 + len(pinned): 0} if had else {},
            scratch_shapes=[
                VMEM((count, STATE, GROUP_LANES), BF16),
                VMEM((count, span, GROUP_LANES), BF16),
                pltpu.SemaphoreType.DMA((count,)),
            ],
            compiler_params=pltpu.CompilerParams(vmem_limit_bytes=12 << 20),
            cost_estimate=takes(1.5),
            name="finish",
        )(info, *pinned, *([y_so_far] if had else []))

    def final_states(after):
        initial, decays = started
        ahead = {}
        for k in range(1, toks):
            i = where[k * unit // GROUP_LANES]
            for part in range(parts):
                ahead[k, part] = received[i * parts + part + HOP * (k - 1)]
        keys = list(ahead)
        ins = [decays, initial, arrived[-1], *ahead.values(), *(states[c] for c in range(chunks))]
        n_after = len(after)

        def kernel(ids_ref, *refs):
            decays_ref, initial_ref, later_ref = refs[:3]
            ahead_refs = dict(zip(keys, refs[3 : 3 + len(keys)]))
            state_refs = refs[3 + len(keys) : 3 + len(keys) + chunks]
            final_ref, buf, sems = refs[-4:][:1] + refs[-2:]
            refs[-3][...] = jnp.zeros_like(refs[-3])

            def branch(device):
                first = device * unit
                group, low = first // GROUP_LANES, first % GROUP_LANES
                lanes = slice(low, low + unit)
                for r in range(requests):
                    part, j = r // REQ_CHUNK, r % REQ_CHUNK
                    value = state_refs[where[group] * parts + part][j, :, lanes].astype(F32)
                    value = value + decay_of(decays_ref, BEFORE_THROUGH, r, group, lanes) * initial_ref[r].astype(F32)
                    if device:
                        through = decay_of(decays_ref, THROUGH, r, group, lanes)
                        value = value + through * ahead_refs[device, part][j, :, lanes].astype(F32)
                    value = value * decay_of(decays_ref, AFTER, r, group, lanes)
                    if device < toks - 1:
                        value = value + later_ref[r].astype(F32)
                    buf[r] = value.T

            on_device(ids_ref[0], toks, branch)
            copies = [pltpu.make_async_copy(buf.at[r], final_ref.at[r], sems.at[r]) for r in range(requests)]
            for copy in copies:
                copy.start()
            for copy in copies:
                copy.wait()

        pinned = [pin(a) for a in (*ins, *after)]
        final, token = pl.pallas_call(
            kernel,
            out_shape=(jax.ShapeDtypeStruct((requests, unit, STATE), F32), VMEM((8, PAIR_LANES), F32)),
            in_specs=[pl.BlockSpec(memory_space=SMEM)] + [pl.BlockSpec(memory_space=VMEM)] * len(pinned),
            out_specs=(any_spec, vmem_spec),
            scratch_shapes=[VMEM((requests, unit, STATE), F32), pltpu.SemaphoreType.DMA((requests,))],
            compiler_params=pltpu.CompilerParams(vmem_limit_bytes=12 << 20),
            cost_estimate=takes(2.7),
            name="final_states",
        )(info, *pinned)
        return final.reshape(requests, unit // HEAD_DIM, HEAD_DIM, STATE), token

    slots = chunks + HOP * (toks - 2)
    lag = HOP * (toks - 2) + parts
    started = []

    def start_parents(previous):
        initial = pl.pallas_call(
            lambda *refs: parents_body(requests, *refs[: 5 + len(pieces)], *refs[6 + len(pieces) :]),
            out_shape=VMEM((requests, STATE, unit), BF16),
            in_specs=[smem_spec] * 4 + [hbm_spec] + [vmem_spec] * (len(pieces) + 1),
            out_specs=vmem_spec,
            scratch_shapes=[VMEM((requests, unit, STATE), F32), pltpu.SemaphoreType.DMA((requests,))],
            compiler_params=pltpu.CompilerParams(vmem_limit_bytes=12 << 20),
            cost_estimate=takes(0.5),
            name="parents",
        )(info, parent, state_dev, state_slot, cache_rows, *pieces, pin(previous))
        decays = call(
            decay_body,
            ((4, requests, 1, width), F32),
            (*all_dt, bias, rates),
            scalars=(info,),
            after=(initial,),
            name="decays",
            us=0.4,
        )
        started.extend((initial, decays))
        send_down(0)
        return decays

    local = {}
    previous = c_flat
    merges_early = any(chain_lanes(order[h // parts], 0, unit) is not None for h in range(min(HOP, chunks)))
    if merges_early:
        previous = start_parents(previous)
    for h in range(HOP):
        send_up(h)
    if groups > 1:
        previous = find_states(1, (previous,))
    pending = list(range(groups))
    downs = list(range(1, toks))
    y_out, done, final = None, 0, None
    for h in range(HOP, slots):
        previous = send_up(h, (previous,))
        if downs and h >= round(HOP + (3 + 2 * (toks - 1 - len(downs))) * parts / 2):
            previous = send_down(downs.pop(0), (previous,))
        if h == HOP:
            if not started:
                previous = start_parents(previous)
            for i in range(2, groups):
                previous = find_states(i, (previous,))
        elif pending:
            i = pending.pop(0)
            local[i] = local_sums(i, (previous,))
            previous = local[i][0]
        elif done < groups - 1 and done * parts + lag + 1 <= h:
            y_out, previous = finish(done, list(range(parts)), y_out, (previous,))
            done += 1
    for s in downs:
        previous = send_down(s, (previous,))
    while pending:
        i = pending.pop(0)
        local[i] = local_sums(i, (previous,))
        previous = local[i][0]
    while done < groups - 1:
        y_out, previous = finish(done, list(range(parts)), y_out, (previous,))
        done += 1
    for part in range(parts):
        if part == parts - 1:
            final, previous = final_states((previous,))
        y_out, previous = finish(groups - 1, [part], y_out, (previous,))
    return (y_out, final)


def solution(mesh):
    placed = (
        P(("groups", "rep"), "tok", "cache"),
        P(("groups", "rep"), "tok", "cache"),
        P(("groups", "rep"), "tok", "cache", None),
        P(("groups", "rep"), "tok", "cache", None),
        P(("groups", "rep"), "tok", "cache"),
        P("cache"),
        P("cache"),
        P("cache"),
        P("cache"),
        P(("groups", "cache"), None, "tok", None, None),
        P("groups"),
        P("groups"),
        P("groups"),
        P("groups"),
    )
    return jax.shard_map(
        shards,
        mesh=mesh,
        in_specs=placed,
        out_specs=(
            P(("groups", "rep"), "tok", "cache"),
            P(("groups", "rep"), ("cache", "tok"), None, None),
        ),
        check_vma=False,
    )
```
